512 devices in a mesh: grid: 128 (over y, z, core), bundle: 4 (over x).
Axes of the slice: x: 4, y: 4, z: 16, core: 2. Of those that a mesh axis runs over, the one named last changes fastest.
Arguments:
- cell_state: float32 [24, 524288], P(None, 'grid'), may hold values from -6 to 6
- pore_volume: float32 [524288], P('grid'), may hold values from 0.5 to 5
- request_cell: int32 [4, 128, 128, 32], P(None, 'grid'), may hold values from 0 to 4095, as said below
- node_slot: int32 [4, 256, 2048], P('bundle', 'grid'), may hold values from 0 to 4095, as said below
- line_length: int32 [4, 256], P('bundle', 'grid'), may hold values from 128 to 2048, as said below
- courant: float32 [4, 256, 2048], P('bundle', 'grid'), may hold values from 0.3 to 3
- flux_weight: float32 [4, 256, 2048], P('bundle', 'grid'), may hold values from 0.3 to 3
- inflow: float32 [4, 24], P('bundle'), may hold values from -4 to 4
- interaction: float32 [24, 24], replicated, may hold values from -0.18 to 0.18
Outputs:
- new_state: float32 [24, 524288], P(None, 'grid')
The draws below stay inside these ranges and needn't reach their ends.
Inputs may be any that keep to these rules, and one draw needn't show every extreme that they name: `request_cell`: a cell owner's local cell index; one entry is the last cell. `node_slot`: an index into the 4096 slots of the device that holds the streamline, slot o * 32 + c belonging to owner o; the last slot is used. `line_length`: live nodes come first on each streamline; some streamline has 2048 and some has 128.
All inputs are finite; a program needn't handle non-finite values.
Results may differ from the reference program's by a relative error of at most 0.0001.
Values sent between devices are 32-bit elements; how exact they have to be, the bound alone decides.
A program may use at most 64 MiB of HBM per device.

```python
import math
import jax
import jax.numpy as jnp
from jax import lax

SPECIES = 24
CELLS_DEV = 4096
LINES_DEV = 2
NODES = 2048
CAP = 32
SUB = 2
NEWTON = 3
MIN_NODES = 128
OWNERS = 128
BUNDLES = 4
SLOTS = 4096
LINES = 256
CELLS = 524288


def draw_request_cell(key, part):
    values = jax.random.randint(key, (BUNDLES, OWNERS, OWNERS, CAP), 0, CELLS_DEV, dtype=jnp.int32)
    return values.at[0, 0, 0, 0].set(CELLS_DEV - 1)


def draw_node_slot(key, part):
    values = jax.random.randint(key, (BUNDLES, LINES, NODES), 0, SLOTS, dtype=jnp.int32)
    return values.at[0, 0, 0].set(SLOTS - 1)


def draw_line_length(key, part):
    first = jax.random.randint(jax.random.fold_in(key, 11), (BUNDLES, LINES), MIN_NODES, NODES + 1, dtype=jnp.int32)
    second = jax.random.randint(jax.random.fold_in(key, 12), (BUNDLES, LINES), MIN_NODES, NODES + 1, dtype=jnp.int32)
    values = jnp.minimum(first, second)
    values = values.at[:, 0].set(NODES)
    return values.at[:, 1].set(MIN_NODES)


def levels(rng, dims, shards, low, high):
    def one(dim, blocks):
        steps = jax.random.uniform(jax.random.fold_in(jax.random.fold_in(rng, 6), dim), (blocks,), jnp.float32, low / len(shards), high / len(shards))
        return jnp.repeat(jnp.exp(steps), dims[dim] // blocks).reshape((-1,) + (1,) * (len(dims) - dim - 1))

    gain = one(*shards[0])
    for cut in shards[1:]:
        gain = gain * one(*cut)
    return gain


def centred(own_key, shape, scale, reach, cuts=(), held_as=jnp.bfloat16):
    entries = jax.random.normal(own_key, shape, jnp.float32) * scale
    if len(cuts) > 0:
        entries = levels(own_key, shape, cuts, -0.22, 0.18) * entries
    return jnp.clip(entries, min=-reach, max=reach).astype(held_as)


def setup_inputs(seed: int = 0) -> dict:
    splits = jax.random.split(jax.random.key(seed), 10)
    cell_state = centred(splits[0], (SPECIES, CELLS), 1.0, 6.0, ((1, 128),), jnp.float32)
    pore_volume = jnp.clip(jnp.exp(math.log(5.0) - 2.3025851 * jax.random.uniform(splits[1], (CELLS,), jnp.float32) ** levels(splits[1], (CELLS,), ((0, 128),), -0.2, 0.2)), 0.5, 5.0)
    request_cell = draw_request_cell(jax.random.fold_in(splits[9], 71), 0)
    node_slot = draw_node_slot(jax.random.fold_in(splits[9], 71), 0)
    line_length = draw_line_length(jax.random.fold_in(splits[9], 71), 0)
    courant = jnp.clip(jnp.exp(math.log(3.0) - 2.3025851 * jax.random.uniform(splits[5], (BUNDLES, LINES, NODES), jnp.float32) ** levels(splits[5], (BUNDLES, LINES, NODES), ((0, 4), (1, 128)), -0.2, 0.2)), 0.3, 3.0)
    flux_weight = jnp.clip(jnp.exp(math.log(3.0) - 2.3025851 * jax.random.uniform(splits[6], (BUNDLES, LINES, NODES), jnp.float32) ** levels(splits[6], (BUNDLES, LINES, NODES), ((0, 4), (1, 128)), -0.2, 0.2)), 0.3, 3.0)
    inflow = centred(splits[7], (BUNDLES, SPECIES), 1.0, 4.0, ((0, 4),), jnp.float32)
    interaction = centred(splits[8], (SPECIES, SPECIES), 0.06, 0.18, (), jnp.float32)
    return {"cell_state": cell_state, "pore_volume": pore_volume, "request_cell": request_cell, "node_slot": node_slot, "line_length": line_length, "courant": courant, "flux_weight": flux_weight, "inflow": inflow, "interaction": interaction}


def transport(state, rate, entry):
    decay = rate / (1.0 + rate)
    source = state / (1.0 + rate)

    def advance(carry, pieces):
        value = pieces[0] * carry + pieces[1]
        return value, value

    initial = jnp.broadcast_to(entry[:, None], state.shape[:2]).astype(jnp.float32)
    final, values = lax.scan(advance, initial, (decay.T, jnp.transpose(source, (2, 0, 1))))
    return jnp.transpose(values, (1, 2, 0))


def speciate(base, interaction):
    iterate = base
    for step in range(NEWTON):
        iterate = base - jnp.dot(interaction, jnp.tanh(iterate), precision=lax.Precision.HIGHEST)
    return iterate


def reference(cell_state, pore_volume, request_cell, node_slot, line_length, courant, flux_weight, inflow, interaction):
    owners = request_cell.shape[1]
    capacity = request_cell.shape[3]
    species = cell_state.shape[0]
    total_cells = cell_state.shape[1]
    offsets = (jnp.arange(owners * capacity, dtype=jnp.int32) // capacity) * (total_cells // owners)
    slot_cell = jnp.transpose(request_cell, (0, 2, 1, 3)).reshape(BUNDLES, owners * owners * capacity)
    slot_cell = slot_cell + jnp.tile(offsets, owners)[None, :]
    weighted_total = jnp.zeros((species, total_cells), jnp.float32)
    flux_total = jnp.zeros((total_cells,), jnp.float32)
    line_device = jnp.arange(LINES, dtype=jnp.int32) // LINES_DEV
    positions = jnp.arange(NODES, dtype=jnp.int32)
    for bundle in range(BUNDLES):
        flat_index = (line_device[:, None] * (owners * capacity) + node_slot[bundle]).astype(jnp.int32)
        node_cell = slot_cell[bundle][flat_index]
        state = cell_state[:, node_cell]
        for substep in range(SUB):
            state = transport(state, courant[bundle], inflow[bundle])
        result = speciate(state.reshape(species, -1), interaction)
        live_mask = positions[None, :] < line_length[bundle][:, None]
        weight = jnp.where(live_mask, flux_weight[bundle], 0.0).reshape(-1)
        flat_cell = node_cell.reshape(-1)
        weighted_total = weighted_total.at[:, flat_cell].add(result * weight[None, :])
        flux_total = flux_total.at[flat_cell].add(weight)
    return (pore_volume[None, :] * cell_state + weighted_total) / (pore_volume[None, :] + flux_total[None, :])
```

```python
import jax
import jax.numpy as jnp
from jax import lax
from jax.experimental import pallas as pl
from jax.experimental.pallas import tpu as pltpu
from jax.sharding import PartitionSpec as P

SUB = 2
NEWTON = 3
SPECIES = 24
CELLS = 4096
SLOTS = 4096
NODES = 2048
LINES = 2
GRID = 128
BUNDLES = 4
CAP = 32
CHUNKS = 64
STEPS = NODES // CHUNKS
TILES = 32
LANES = 128
LOW = 256
HIGH = 16
QUARTER = CELLS // BUNDLES
MESH = pl.DeviceIdType.MESH


def lane_ids(rows):
    return lax.broadcasted_iota(jnp.int32, (rows, LANES), 1)


def row_ids(rows=8):
    return lax.broadcasted_iota(jnp.int32, (rows, LANES), 0)


def swap_blocks(parts):
    lane = lane_ids(parts[0].shape[0])
    far = lane < 64
    near = (lane & 32) == 0
    a, b, c, d = parts
    a, c = jnp.where(far, a, pltpu.roll(c, 64, 1)), jnp.where(far, pltpu.roll(a, 64, 1), c)
    b, d = jnp.where(far, b, pltpu.roll(d, 64, 1)), jnp.where(far, pltpu.roll(b, 64, 1), d)
    a, b = jnp.where(near, a, pltpu.roll(b, 32, 1)), jnp.where(near, pltpu.roll(a, 96, 1), b)
    c, d = jnp.where(near, c, pltpu.roll(d, 32, 1)), jnp.where(near, pltpu.roll(c, 96, 1), d)
    return a, b, c, d


def to_groups(v0, v1, v2):
    row = row_ids()
    last = jnp.where(
        row < 2,
        pltpu.roll(v0, 2, 0),
        jnp.where(row < 4, pltpu.roll(v1, 4, 0), pltpu.roll(v2, 6, 0)),
    )
    return v0, v1, v2, last


def from_groups(g0, g1, g2, g3):
    row = row_ids()
    low = row < 6
    return (
        jnp.where(low, g0, pltpu.roll(g3, 6, 0)),
        jnp.where(low, g1, pltpu.roll(g3, 4, 0)),
        jnp.where(low, g2, pltpu.roll(g3, 2, 0)),
    )


def gather_tile(load, index):
    lane = jnp.broadcast_to(index & 127, (8, LANES))
    tile = jnp.broadcast_to(index >> 7, (8, LANES))
    found = [jnp.zeros((8, LANES), jnp.float32)] * 3
    for k in range(TILES):
        here = tile == k
        for g in range(3):
            found[g] = jnp.where(here, jnp.take_along_axis(load(k, g), lane, axis=1), found[g])
    return found


def scatter_sums(rows_ref, index_ref, acc_ref):
    width = 512
    acc_ref[...] = jnp.zeros_like(acc_ref)

    def step(j, _):
        off = pl.multiple_of(j * width, width)
        index = index_ref[:, pl.ds(off, width)]
        rows = rows_ref[:, pl.ds(off, width)]
        top = rows.astype(jnp.bfloat16).astype(jnp.float32)
        rest = rows - top
        high = index >> 8
        tops = []
        rests = []
        for k in range(HIGH):
            here = jnp.broadcast_to(high == k, (32, width))
            tops.append(jnp.where(here, top, 0.0).astype(jnp.bfloat16))
            rests.append(jnp.where(here, rest, 0.0).astype(jnp.bfloat16))
        left = jnp.concatenate([jnp.concatenate(tops, 0), jnp.concatenate(rests, 0)], 1)
        low = jnp.broadcast_to(index & (LOW - 1), (LOW, width))
        hot = lax.broadcasted_iota(jnp.int32, (LOW, width), 0) == low
        hot = hot.astype(jnp.float32).astype(jnp.bfloat16)
        right = jnp.concatenate([hot, hot], 1)
        acc_ref[...] += lax.dot_general(
            left, right, (((1,), (1,)), ((), ())), preferred_element_type=jnp.float32
        )
        return 0

    lax.fori_loop(0, rows_ref.shape[1] // width, step, 0)


def kernel(
    cell_ref,
    pore_ref,
    request_ref,
    slot_ref,
    courant_ref,
    weight_ref,
    inflow_ref,
    inter_ref,
    out_ref,
    send1,
    recv1,
    send2,
    recv2,
    table,
    state,
    rows,
    acc,
    part,
    part_flux,
    got,
    got_flux,
    own_sem,
    send1_sem,
    recv1_sem,
    send2_sem,
    recv2_sem,
    send3_sem,
    recv3_sem,
    send4_sem,
    recv4_sem,
    send5_sem,
    recv5_sem,
):
    me = lax.axis_index("grid")
    mine = lax.axis_index("bundle")

    barrier = pltpu.get_barrier_semaphore()

    def greet(k, _):
        pl.semaphore_signal(
            barrier, inc=1, device_id=(lax.rem(me + k, GRID), mine), device_id_type=MESH
        )
        return 0

    lax.fori_loop(1, GRID, greet, 0)
    for k in range(1, BUNDLES):
        pl.semaphore_signal(
            barrier, inc=1, device_id=(me, lax.rem(mine + k, BUNDLES)), device_id_type=MESH
        )

    def pick(t, _):
        index = request_ref[:, pl.ds(pl.multiple_of(t * LANES, LANES), LANES)]
        found = gather_tile(
            lambda k, g: cell_ref[8 * g : 8 * g + 8, k * LANES : (k + 1) * LANES], index
        )
        blocks = swap_blocks(to_groups(*found))
        for d in range(4):
            send1[t * 4 + d] = blocks[d][:6]
        return 0

    lax.fori_loop(0, TILES, pick, 0)
    pl.semaphore_wait(barrier, GRID - 1 + BUNDLES - 1)

    def exchange(source, target, send_sem, recv_sem):
        def post(k, _):
            peer = lax.rem(me + k, GRID)
            pltpu.make_async_remote_copy(
                src_ref=source.at[peer],
                dst_ref=target.at[me],
                send_sem=send_sem,
                recv_sem=recv_sem,
                device_id=(peer, mine),
                device_id_type=MESH,
            ).start()
            return 0

        lax.fori_loop(1, GRID, post, 0)
        own = pltpu.make_async_copy(source.at[me], target.at[me], own_sem)
        own.start()
        own.wait()

    def settle(source, target, send_sem, recv_sem):
        rest = pl.ds(0, GRID - 1)
        pltpu.make_async_copy(target.at[rest], target.at[rest], recv_sem).wait()
        pltpu.make_async_copy(source.at[rest], source.at[rest], send_sem).wait()

    exchange(send1, recv1, send1_sem, recv1_sem)
    settle(send1, recv1, send1_sem, recv1_sem)

    def unpack(t, _):
        pad = jnp.zeros((2, LANES), jnp.float32)
        parts = swap_blocks([jnp.concatenate([recv1[t * 4 + d], pad], 0) for d in range(4)])
        for g, value in enumerate(from_groups(*parts)):
            table[t, 8 * g : 8 * g + 8, :] = value
        return 0

    lax.fori_loop(0, TILES, unpack, 0)

    def fetch(t, _):
        index = slot_ref[:, pl.ds(pl.multiple_of(t * LANES, LANES), LANES)]
        found = gather_tile(lambda k, g: table[k, 8 * g : 8 * g + 8, :], index)
        for g in range(3):
            state[t, 8 * g : 8 * g + 8, :] = found[g]
        return 0

    lax.fori_loop(0, TILES, fetch, 0)

    chunk = lane_ids(SPECIES) & (CHUNKS - 1)
    entry = inflow_ref[...]

    def rate(i):
        return courant_ref[:, i * LANES : (i + 1) * LANES]

    scales = []
    decays = []
    spans = []
    for i in range(STEPS):
        scale = 1.0 / (1.0 + rate(i))
        decay = rate(i) * scale
        scales.append(jnp.broadcast_to(scale, (8, LANES)))
        decays.append(jnp.broadcast_to(decay, (8, LANES)))
        spans.append(decays[0] if i == 0 else spans[-1] * decays[i])
    wide = [[jnp.concatenate([x] * 3, 0) for x in xs] for xs in (scales, decays, spans)]
    scales, decays, spans = wide
    levels = []
    level = spans[-1]
    for bit in range(6):
        levels.append(level)
        behind = pltpu.roll(level, 1 << bit, 1)
        level = jnp.where(chunk >= (1 << bit), level * behind, level)
    for substep in range(SUB):
        value = jnp.zeros((SPECIES, LANES), jnp.float32)
        for i in range(STEPS):
            value = decays[i] * value + scales[i] * state[i]
            state[i] = value
        ends = jnp.where(chunk == 0, value + spans[-1] * entry, value)
        for bit in range(6):
            behind = pltpu.roll(ends, 1 << bit, 1)
            ends = jnp.where(chunk >= (1 << bit), ends + levels[bit] * behind, ends)
        before = jnp.where(chunk == 0, entry, pltpu.roll(ends, 1, 1))
        for i in range(STEPS):
            state[i] = state[i] + spans[i] * before

    inter = inter_ref[...]

    def react(j, _):
        base = jnp.concatenate([state[j * 4 + q] for q in range(4)], 1)
        iterate = base
        for _step in range(NEWTON):
            iterate = base - jnp.dot(
                inter,
                jnp.tanh(iterate),
                precision=lax.Precision.HIGHEST,
                preferred_element_type=jnp.float32,
            )
        for q in range(4):
            off = pl.multiple_of((j * 4 + q) * LANES, LANES)
            weight = jnp.broadcast_to(weight_ref[:, pl.ds(off, LANES)], (8, LANES))
            result = iterate[:, q * LANES : (q + 1) * LANES]
            groups = to_groups(*[result[8 * g : 8 * g + 8] * weight for g in range(3)])
            groups = (jnp.where(row_ids() == 6, weight, groups[0]),) + groups[1:]
            for g in range(4):
                rows[8 * g : 8 * g + 8, pl.ds(off, LANES)] = groups[g]
        return 0

    lax.fori_loop(0, TILES // 4, react, 0)
    scatter_sums(rows, slot_ref, acc)

    def pack(h, _):
        for half in range(2):
            parts = [
                acc[pl.ds(pl.multiple_of(h * 32 + 8 * g, 8), 8), half * LANES : (half + 1) * LANES]
                for g in range(4)
            ]
            blocks = swap_blocks(parts)
            for d in range(4):
                send2[h * 8 + half * 4 + d] = blocks[d][:7]
        return 0

    lax.fori_loop(0, HIGH, pack, 0)
    exchange(send2, recv2, send2_sem, recv2_sem)
    settle(send2, recv2, send2_sem, recv2_sem)

    def unpack_back(t, _):
        off = pl.multiple_of(t * LANES, LANES)
        pad = jnp.zeros((1, LANES), jnp.float32)
        parts = swap_blocks([jnp.concatenate([recv2[t * 4 + d], pad], 0) for d in range(4)])
        for g in range(4):
            rows[8 * g : 8 * g + 8, pl.ds(off, LANES)] = parts[g]
        return 0

    lax.fori_loop(0, TILES, unpack_back, 0)
    scatter_sums(rows, request_ref, acc)

    for h in range(HIGH):
        for half in range(2):
            lanes = slice(half * LANES, (half + 1) * LANES)
            groups = [acc[h * 32 + 8 * g : h * 32 + 8 * g + 8, lanes] for g in range(4)]
            cells = slice((h * 2 + half) * LANES, (h * 2 + half + 1) * LANES)
            for g, value in enumerate(from_groups(*groups)):
                part[8 * g : 8 * g + 8, cells] = value
            part_flux[:, cells] = groups[0][6:7]

    posts = []
    for k in range(1, BUNDLES):
        peer = lax.rem(mine + k, BUNDLES)
        cells = pl.ds(pl.multiple_of(peer * QUARTER, QUARTER), QUARTER)
        for source, target, sends, recvs in (
            (part, got, send3_sem, recv3_sem),
            (part_flux, got_flux, send4_sem, recv4_sem),
        ):
            copy = pltpu.make_async_remote_copy(
                src_ref=source.at[:, cells],
                dst_ref=target.at[k - 1],
                send_sem=sends.at[k - 1],
                recv_sem=recvs.at[k - 1],
                device_id=(me, peer),
                device_id_type=MESH,
            )
            copy.start()
            posts.append(copy)
    for copy in posts:
        copy.wait()
    ours = pl.ds(pl.multiple_of(mine * QUARTER, QUARTER), QUARTER)
    total = part[:, ours] + got[0] + got[1] + got[2]
    flux = part_flux[:, ours] + got_flux[0] + got_flux[1] + got_flux[2]
    pore = pore_ref[:, ours]
    out_ref[:, ours] = (pore * cell_ref[:, ours] + total) / (pore + flux)
    posts = []
    for k in range(1, BUNDLES):
        copy = pltpu.make_async_remote_copy(
            src_ref=out_ref.at[:, ours],
            dst_ref=out_ref.at[:, ours],
            send_sem=send5_sem.at[k - 1],
            recv_sem=recv5_sem.at[k - 1],
            device_id=(me, lax.rem(mine + k, BUNDLES)),
            device_id_type=MESH,
        )
        copy.start()
        posts.append(copy)
    for copy in posts:
        copy.wait()


def by_step(values):
    return values.reshape(LINES, CHUNKS, STEPS).transpose(2, 0, 1).reshape(1, LINES * NODES)


def shards(
    cell_state,
    pore_volume,
    request_cell,
    node_slot,
    line_length,
    courant,
    flux_weight,
    inflow,
    interaction,
):
    request = lax.dynamic_index_in_dim(
        request_cell[:, 0], lax.axis_index("bundle"), 0, keepdims=False
    ).reshape(1, SLOTS)
    positions = lax.broadcasted_iota(jnp.int32, (LINES, NODES), 1)
    weight = jnp.where(positions < line_length[0][:, None], flux_weight[0], 0.0)
    entry = jnp.broadcast_to(inflow[0][:, None], (SPECIES, LANES))
    vmem = pl.BlockSpec(memory_space=pltpu.VMEM)
    f32 = jnp.float32
    dma = pltpu.SemaphoreType.DMA
    return pl.pallas_call(
        kernel,
        out_shape=jax.ShapeDtypeStruct((SPECIES, CELLS), f32),
        in_specs=[vmem] * 8,
        out_specs=vmem,
        scratch_shapes=[
            pltpu.VMEM((GRID, 6, LANES), f32),
            pltpu.VMEM((GRID, 6, LANES), f32),
            pltpu.VMEM((GRID, 7, LANES), f32),
            pltpu.VMEM((GRID, 7, LANES), f32),
            pltpu.VMEM((TILES, SPECIES, LANES), f32),
            pltpu.VMEM((TILES, SPECIES, LANES), f32),
            pltpu.VMEM((32, SLOTS), f32),
            pltpu.VMEM((HIGH * 32, LOW), f32),
            pltpu.VMEM((SPECIES, CELLS), f32),
            pltpu.VMEM((1, CELLS), f32),
            pltpu.VMEM((BUNDLES - 1, SPECIES, QUARTER), f32),
            pltpu.VMEM((BUNDLES - 1, 1, QUARTER), f32),
            dma,
            dma,
            dma,
            dma,
            dma,
            dma((3,)),
            dma((3,)),
            dma((3,)),
            dma((3,)),
            dma((3,)),
            dma((3,)),
        ],
        compiler_params=pltpu.CompilerParams(collective_id=0, has_side_effects=True),
        name="streamlines",
    )(
        cell_state,
        pore_volume.reshape(1, CELLS),
        request,
        by_step(node_slot),
        by_step(courant),
        by_step(weight),
        entry,
        interaction,
    )


def solution(mesh):
    placed = (
        P(None, "grid"),
        P("grid"),
        P(None, "grid", None, None),
        P("bundle", "grid", None),
        P("bundle", "grid"),
        P("bundle", "grid", None),
        P("bundle", "grid", None),
        P("bundle", None),
        P(),
    )
    return jax.shard_map(
        shards, mesh=mesh, in_specs=placed, out_specs=P(None, "grid"), check_vma=False
    )
```

```python
import jax
import jax.numpy as jnp
from jax import lax
from jax.experimental import pallas as pl
from jax.experimental.pallas import tpu as pltpu
from jax.sharding import PartitionSpec as P

SUB = 2
NEWTON = 3
SPECIES = 24
CELLS = 4096
SLOTS = 4096
NODES = 2048
LINES = 2
GRID = 128
BUNDLES = 4
CAP = 32
CHUNKS = 64
STEPS = NODES // CHUNKS
TILES = 32
LANES = 128
LOW = 256
HIGH = 16
QUARTER = CELLS // BUNDLES
MESH = pl.DeviceIdType.MESH


def lane_ids(rows):
    return lax.broadcasted_iota(jnp.int32, (rows, LANES), 1)


def row_ids(rows=8):
    return lax.broadcasted_iota(jnp.int32, (rows, LANES), 0)


def swap_blocks(parts):
    lane = lane_ids(parts[0].shape[0])
    far = lane < 64
    near = (lane & 32) == 0
    a, b, c, d = parts
    a, c = jnp.where(far, a, pltpu.roll(c, 64, 1)), jnp.where(far, pltpu.roll(a, 64, 1), c)
    b, d = jnp.where(far, b, pltpu.roll(d, 64, 1)), jnp.where(far, pltpu.roll(b, 64, 1), d)
    a, b = jnp.where(near, a, pltpu.roll(b, 32, 1)), jnp.where(near, pltpu.roll(a, 96, 1), b)
    c, d = jnp.where(near, c, pltpu.roll(d, 32, 1)), jnp.where(near, pltpu.roll(c, 96, 1), d)
    return a, b, c, d


def to_groups(v0, v1, v2):
    row = row_ids()
    last = jnp.where(
        row < 2,
        pltpu.roll(v0, 2, 0),
        jnp.where(row < 4, pltpu.roll(v1, 4, 0), pltpu.roll(v2, 6, 0)),
    )
    return v0, v1, v2, last


def from_groups(g0, g1, g2, g3):
    row = row_ids()
    low = row < 6
    return (
        jnp.where(low, g0, pltpu.roll(g3, 6, 0)),
        jnp.where(low, g1, pltpu.roll(g3, 4, 0)),
        jnp.where(low, g2, pltpu.roll(g3, 2, 0)),
    )


def gather_tile(load, index, count, found):
    lane = jnp.broadcast_to(index & 127, (8, LANES))
    tile = jnp.broadcast_to(index >> 7, (8, LANES))
    for k in range(count):
        here = tile == k
        for g in range(3):
            found[g] = jnp.where(here, jnp.take_along_axis(load(k, g), lane, axis=1), found[g])
    return found


def expand(tiles, indices, highs):
    tops = []
    rests = []
    for tile, index in zip(tiles, indices):
        top = tile.astype(jnp.bfloat16).astype(jnp.float32)
        rest = tile - top
        high = jnp.broadcast_to(index >> 8, (32, LANES))
        column = [[], []]
        for k in highs:
            here = high == k
            column[0].append(jnp.where(here, top, 0.0).astype(jnp.bfloat16))
            column[1].append(jnp.where(here, rest, 0.0).astype(jnp.bfloat16))
        tops.append(jnp.concatenate(column[0], 0))
        rests.append(jnp.concatenate(column[1], 0))
    return jnp.concatenate(tops + rests, 1)


def hot_tile(index):
    low = jnp.broadcast_to(index & (LOW - 1), (LOW, LANES))
    hot = lax.broadcasted_iota(jnp.int32, (LOW, LANES), 0) == low
    return hot.astype(jnp.float32).astype(jnp.bfloat16)


def contract(left, hots):
    right = jnp.concatenate(hots + hots, 1)
    return lax.dot_general(
        left, right, (((1,), (1,)), ((), ())), preferred_element_type=jnp.float32
    )


def side_by_side(blocks):
    lane = lane_ids(32)
    out = blocks[0]
    for j in range(1, 4):
        out = jnp.where(lane >= 32 * j, pltpu.roll(blocks[j], 32 * j, 1), out)
    return out


def by_step(source_ref, lines_ref, square_ref):
    for m in range(16):
        lines_ref[2 * m : 2 * m + 2, :] = source_ref[:, m * LANES : (m + 1) * LANES]
    square_ref[:, 0:32] = jnp.transpose(lines_ref[...], (1, 0))
    mixed = side_by_side([square_ref[32 * q : 32 * q + 32, :] for q in range(4)])
    lane = lane_ids(8)
    take = (lane & 3) * 32 + ((lane >> 2) & 15) * 2 + (lane >> 6)
    return jnp.concatenate(
        [jnp.take_along_axis(mixed[8 * j : 8 * j + 8], take, axis=1) for j in range(4)], 0
    )


ORDER = (2, 1, 3, 0)


def kernel(
    cell_hbm,
    pore_hbm,
    request_hbm,
    slot_hbm,
    length_hbm,
    courant_hbm,
    weight_hbm,
    inflow_hbm,
    inter_hbm,
    out_ref,
    cell_ref,
    pore_ref,
    request_in,
    slot_in,
    length_in,
    courant_in,
    weight_in,
    inflow_in,
    inter_in,
    square_i,
    square_f,
    lines_i,
    lines_f,
    request_ref,
    slot_ref,
    weight_ref,
    scale_ref,
    decay_ref,
    span_ref,
    hot_slot,
    hot_request,
    send1,
    recv1,
    send2,
    recv2,
    table,
    state,
    rows,
    acc,
    part,
    part_flux,
    got,
    got_flux,
    in_sem,
    own_sem,
    send1_sem,
    recv1_sem,
    send2_sem,
    recv2_sem,
    send3_sem,
    recv3_sem,
    send4_sem,
    recv4_sem,
    send5_sem,
    recv5_sem,
):
    me = lax.axis_index("grid")
    mine = lax.axis_index("bundle")
    my_y = lax.div(me, 32)
    my_z = lax.rem(lax.div(me, 2), 16)
    my_core = lax.rem(me, 2)

    loads = [
        pltpu.make_async_copy(source, target, in_sem.at[j])
        for j, (source, target) in enumerate(
            (
                (request_hbm.at[mine], request_in),
                (cell_hbm, cell_ref),
                (slot_hbm, slot_in),
                (courant_hbm, courant_in),
                (weight_hbm, weight_in),
                (length_hbm, length_in),
                (inflow_hbm, inflow_in),
                (inter_hbm, inter_in),
                (pore_hbm, pore_ref),
            )
        )
    ]
    for load in loads:
        load.start()

    barrier = pltpu.get_barrier_semaphore()

    def greet(k, _):
        pl.semaphore_signal(
            barrier, inc=1, device_id=(lax.rem(me + k, GRID), mine), device_id_type=MESH
        )
        return 0

    lax.fori_loop(1, GRID, greet, 0)
    for k in range(1, BUNDLES):
        pl.semaphore_signal(
            barrier, inc=1, device_id=(me, lax.rem(mine + k, BUNDLES)), device_id_type=MESH
        )

    loads[0].wait()
    square_i[:, 0:32] = jnp.transpose(request_in[...], (1, 0))
    request_ref[...] = side_by_side([square_i[pl.ds(d, 32, stride=4), :] for d in range(4)])
    loads[1].wait()

    def pick(t, _):
        found = gather_tile(
            lambda k, g: cell_ref[8 * g : 8 * g + 8, k * LANES : (k + 1) * LANES],
            request_ref[pl.ds(t, 1), :],
            TILES,
            [jnp.zeros((8, LANES), jnp.float32)] * 3,
        )
        blocks = swap_blocks(to_groups(*found))
        for d in range(4):
            send1[t * 4 + d] = blocks[d][:6]
        return 0

    lax.fori_loop(0, TILES, pick, 0, unroll=2)
    pl.semaphore_wait(barrier, GRID - 1 + BUNDLES - 1)

    def post_one(source, target, send_sem, recv_sem, peer):
        pltpu.make_async_remote_copy(
            src_ref=source.at[peer],
            dst_ref=target.at[me],
            send_sem=send_sem,
            recv_sem=recv_sem,
            device_id=(peer, mine),
            device_id_type=MESH,
        ).start()

    def post(source, target, send_sem, recv_sems, r):
        first = lax.rem(my_y + r, 4) * 32

        def ring(j, _):
            hop = 8 + lax.div(j + 1, 2) * (1 - 2 * lax.rem(j, 2))
            spot = first + lax.rem(my_z + hop, 16) * 2
            for core in range(2):
                post_one(source, target, send_sem, recv_sems.at[r], spot + core)
            return 0

        lax.fori_loop(0, 16 if r else 15, ring, 0)
        if r == 0:
            post_one(
                source, target, send_sem, recv_sems.at[0], first + my_z * 2 + 1 - my_core
            )
            own = pltpu.make_async_copy(source.at[me], target.at[me], own_sem)
            own.start()
            own.wait()

    def arrived(target, recv_sems, r):
        blocks = pl.ds(0, 32 if r else 31)
        pltpu.make_async_copy(target.at[blocks], target.at[blocks], recv_sems.at[r]).wait()
        return lax.rem(my_y + 4 - r, 4)

    def sent(source, send_sem):
        blocks = pl.ds(0, GRID - 1)
        pltpu.make_async_copy(source.at[blocks], source.at[blocks], send_sem).wait()

    for r in ORDER:
        post(send1, recv1, send1_sem, recv1_sem, r)

    for load in loads[2:]:
        load.wait()
    slot_ref[...] = by_step(slot_in, lines_i, square_i)
    courant = by_step(courant_in, lines_f, square_f)
    scale = 1.0 / (1.0 + courant)
    scale_ref[...] = scale
    decay_ref[...] = courant * scale
    span_ref[0:1, :] = decay_ref[0:1, :]
    for i in range(1, STEPS):
        span_ref[i : i + 1, :] = span_ref[i - 1 : i, :] * decay_ref[i : i + 1, :]
    flux = by_step(weight_in, lines_f, square_f)
    lane = lane_ids(32)
    node = (lane & (CHUNKS - 1)) * STEPS + row_ids(32)
    first_line = jnp.broadcast_to(length_in[:, 0:1], (32, LANES))
    second_line = jnp.broadcast_to(length_in[:, 1:2], (32, LANES))
    weight_ref[...] = jnp.where(node < jnp.where(lane < CHUNKS, first_line, second_line), flux, 0.0)

    def heat(t, _):
        hot_slot[t] = hot_tile(slot_ref[pl.ds(t, 1), :])
        hot_request[t] = hot_tile(request_ref[pl.ds(t, 1), :])
        return 0

    lax.fori_loop(0, TILES, heat, 0)
    square = lax.broadcasted_iota(jnp.int32, (SPECIES, SPECIES), 0) == lax.broadcasted_iota(
        jnp.int32, (SPECIES, SPECIES), 1
    )
    entry = jnp.sum(
        jnp.where(square, jnp.broadcast_to(inflow_in[...], (SPECIES, SPECIES)), 0.0),
        axis=1,
        keepdims=True,
    )
    entry = jnp.broadcast_to(entry, (SPECIES, LANES))
    square_f[0:SPECIES, :] = jnp.zeros((SPECIES, LANES), jnp.float32)
    square_f[0:SPECIES, 0:SPECIES] = inter_in[...]
    inter = square_f[0:SPECIES, :]
    inter_top = inter.astype(jnp.bfloat16).astype(jnp.float32)
    inter_rest = inter - inter_top
    inter = inter_top + pltpu.roll(inter_top, 32, 1) + pltpu.roll(inter_rest, 64, 1)
    inter = inter.astype(jnp.bfloat16)
    chunk = lane_ids(SPECIES) & (CHUNKS - 1)
    levels = []
    level = jnp.broadcast_to(span_ref[STEPS - 1 : STEPS, :], (SPECIES, LANES))
    span_all = level
    for bit in range(6):
        levels.append(level)
        behind = pltpu.roll(level, 1 << bit, 1)
        level = jnp.where(chunk >= (1 << bit), level * behind, level)

    for step, r in enumerate(ORDER):
        base = arrived(recv1, recv1_sem, r) * 8
        pad = jnp.zeros((2, LANES), jnp.float32)
        for u in range(8):
            parts = [
                jnp.concatenate([recv1[base * 4 + u * 4 + d], pad], 0) for d in range(4)
            ]
            for g, value in enumerate(from_groups(*swap_blocks(parts))):
                table[u, 8 * g : 8 * g + 8, :] = value

        def fetch(t, _, base=base, step=step):
            if step == 0:
                found = [jnp.zeros((8, LANES), jnp.float32)] * 3
            else:
                found = [state[t, 8 * g : 8 * g + 8, :] for g in range(3)]
            found = gather_tile(
                lambda k, g: table[k, 8 * g : 8 * g + 8, :],
                slot_ref[pl.ds(t, 1), :] - base * LANES,
                8,
                found,
            )
            for g in range(3):
                state[t, 8 * g : 8 * g + 8, :] = found[g]
            return 0

        lax.fori_loop(0, TILES, fetch, 0, unroll=4)

    def row(ref, i):
        return jnp.broadcast_to(ref[i : i + 1, :], (SPECIES, LANES))

    for substep in range(SUB):
        value = jnp.zeros((SPECIES, LANES), jnp.float32)
        for i in range(STEPS):
            value = row(decay_ref, i) * value + row(scale_ref, i) * state[i]
            state[i] = value
        ends = jnp.where(chunk == 0, value + span_all * entry, value)
        for bit in range(6):
            behind = pltpu.roll(ends, 1 << bit, 1)
            ends = jnp.where(chunk >= (1 << bit), ends + levels[bit] * behind, ends)
        before = jnp.where(chunk == 0, entry, pltpu.roll(ends, 1, 1))
        for i in range(STEPS):
            state[i] = state[i] + row(span_ref, i) * before

    def react(j, _):
        base = jnp.concatenate([state[j * 4 + q] for q in range(4)], 1)
        gap = jnp.zeros((8, 4 * LANES), jnp.float32)
        iterate = base
        for _step in range(NEWTON):
            active = jnp.concatenate([jnp.tanh(iterate), gap], 0)
            top = active.astype(jnp.bfloat16)
            rest = (active - top.astype(jnp.float32)).astype(jnp.bfloat16)
            stack = jnp.concatenate([top, rest, top, jnp.zeros_like(top)], 0)
            iterate = base - jnp.dot(inter, stack, preferred_element_type=jnp.float32)
        for q in range(4):
            weight = jnp.broadcast_to(weight_ref[pl.ds(j * 4 + q, 1), :], (8, LANES))
            result = iterate[:, q * LANES : (q + 1) * LANES]
            groups = to_groups(*[result[8 * g : 8 * g + 8] * weight for g in range(3)])
            groups = (jnp.where(row_ids() == 6, weight, groups[0]),) + groups[1:]
            for g in range(4):
                rows[j * 4 + q, 8 * g : 8 * g + 8, :] = groups[g]
        return 0

    lax.fori_loop(0, TILES // 4, react, 0, unroll=2)

    sent(send1, send1_sem)
    for half in range(2):
        ys = [lax.rem(my_y + r, 4) for r in ORDER[2 * half : 2 * half + 2]]
        highs = [y * 4 + sub for y in ys for sub in range(4)]
        total = None
        for j in range(TILES // 4):
            span = range(4 * j, 4 * j + 4)
            left = expand([rows[t] for t in span], [slot_ref[t : t + 1, :] for t in span], highs)
            more = contract(left, [hot_slot[t] for t in span])
            if j == 0:
                acc[0:LOW, :] = more
            else:
                acc[0:LOW, :] += more
        for k in range(8):
            for side in range(2):
                lanes = slice(side * LANES, (side + 1) * LANES)
                blocks = swap_blocks(
                    [acc[k * 32 + 8 * g : k * 32 + 8 * g + 8, lanes] for g in range(4)]
                )
                for d in range(4):
                    send2[highs[k] * 8 + side * 4 + d] = blocks[d][:7]
        for r in ORDER[2 * half : 2 * half + 2]:
            post(send2, recv2, send2_sem, recv2_sem, r)

    for step, r in enumerate(ORDER):
        base = arrived(recv2, recv2_sem, r) * 8
        pad = jnp.zeros((1, LANES), jnp.float32)
        indices = request_ref[pl.ds(pl.multiple_of(base, 8), 8), :]
        for j in range(2):
            tiles = []
            for u in range(4 * j, 4 * j + 4):
                parts = [
                    jnp.concatenate([recv2[base * 4 + u * 4 + d], pad], 0) for d in range(4)
                ]
                tiles.append(jnp.concatenate(swap_blocks(parts), 0))
            span = range(4 * j, 4 * j + 4)
            left = expand(tiles, [indices[u : u + 1] for u in span], range(HIGH))
            more = contract(left, [hot_request[base + u] for u in span])
            if step == 0 and j == 0:
                acc[...] = more
            else:
                acc[...] += more

    for h in range(HIGH):
        for half in range(2):
            lanes = slice(half * LANES, (half + 1) * LANES)
            groups = [acc[h * 32 + 8 * g : h * 32 + 8 * g + 8, lanes] for g in range(4)]
            cells = slice((h * 2 + half) * LANES, (h * 2 + half + 1) * LANES)
            for g, value in enumerate(from_groups(*groups)):
                part[8 * g : 8 * g + 8, cells] = value
            part_flux[:, cells] = groups[0][6:7]

    posts = []
    for k in (2, 1, 3):
        peer = lax.rem(mine + k, BUNDLES)
        cells = pl.ds(pl.multiple_of(peer * QUARTER, QUARTER), QUARTER)
        for source, target, sends, recvs in (
            (part, got, send3_sem, recv3_sem),
            (part_flux, got_flux, send4_sem, recv4_sem),
        ):
            copy = pltpu.make_async_remote_copy(
                src_ref=source.at[:, cells],
                dst_ref=target.at[k - 1],
                send_sem=sends.at[k - 1],
                recv_sem=recvs.at[k - 1],
                device_id=(me, peer),
                device_id_type=MESH,
            )
            copy.start()
            posts.append(copy)
    sent(send2, send2_sem)
    for copy in posts:
        copy.wait()
    ours = pl.ds(pl.multiple_of(mine * QUARTER, QUARTER), QUARTER)
    total = part[:, ours] + got[0] + got[1] + got[2]
    flux = part_flux[:, ours] + got_flux[0] + got_flux[1] + got_flux[2]
    pore = pore_ref[:, ours]
    out_ref[:, ours] = (pore * cell_ref[:, ours] + total) / (pore + flux)
    posts = []
    for k in (2, 1, 3):
        copy = pltpu.make_async_remote_copy(
            src_ref=out_ref.at[:, ours],
            dst_ref=out_ref.at[:, ours],
            send_sem=send5_sem.at[k - 1],
            recv_sem=recv5_sem.at[k - 1],
            device_id=(me, lax.rem(mine + k, BUNDLES)),
            device_id_type=MESH,
        )
        copy.start()
        posts.append(copy)
    for copy in posts:
        copy.wait()


def shards(
    cell_state,
    pore_volume,
    request_cell,
    node_slot,
    line_length,
    courant,
    flux_weight,
    inflow,
    interaction,
):
    f32 = jnp.float32
    i32 = jnp.int32
    vmem = pltpu.VMEM
    dma = pltpu.SemaphoreType.DMA
    return pl.pallas_call(
        kernel,
        out_shape=jax.ShapeDtypeStruct((SPECIES, CELLS), f32),
        in_specs=[pl.BlockSpec(memory_space=pl.ANY)] * 9,
        out_specs=pl.BlockSpec(memory_space=pltpu.VMEM),
        scratch_shapes=[
            vmem((SPECIES, CELLS), f32),
            vmem((1, CELLS), f32),
            vmem((CAP, GRID), i32),
            vmem((LINES, NODES), i32),
            vmem((1, LINES), i32),
            vmem((LINES, NODES), f32),
            vmem((LINES, NODES), f32),
            vmem((1, SPECIES), f32),
            vmem((SPECIES, SPECIES), f32),
            vmem((LANES, LANES), i32),
            vmem((LANES, LANES), f32),
            vmem((32, LANES), i32),
            vmem((32, LANES), f32),
            vmem((32, LANES), i32),
            vmem((32, LANES), i32),
            vmem((32, LANES), f32),
            vmem((32, LANES), f32),
            vmem((32, LANES), f32),
            vmem((32, LANES), f32),
            vmem((TILES, LOW, LANES), jnp.bfloat16),
            vmem((TILES, LOW, LANES), jnp.bfloat16),
            vmem((GRID, 6, LANES), f32),
            vmem((GRID, 6, LANES), f32),
            vmem((GRID, 7, LANES), f32),
            vmem((GRID, 7, LANES), f32),
            vmem((8, SPECIES, LANES), f32),
            vmem((TILES, SPECIES, LANES), f32),
            vmem((TILES, 32, LANES), f32),
            vmem((HIGH * 32, LOW), f32),
            vmem((SPECIES, CELLS), f32),
            vmem((1, CELLS), f32),
            vmem((BUNDLES - 1, SPECIES, QUARTER), f32),
            vmem((BUNDLES - 1, 1, QUARTER), f32),
            dma((9,)),
            dma,
            dma,
            dma((4,)),
            dma,
            dma((4,)),
            dma((3,)),
            dma((3,)),
            dma((3,)),
            dma((3,)),
            dma((3,)),
            dma((3,)),
        ],
        compiler_params=pltpu.CompilerParams(collective_id=0, has_side_effects=True),
        name="streamlines",
    )(
        cell_state,
        pore_volume.reshape(1, CELLS),
        jnp.transpose(request_cell[:, 0], (0, 2, 1)),
        node_slot[0],
        line_length,
        courant[0],
        flux_weight[0],
        inflow,
        interaction,
    )


def solution(mesh):
    placed = (
        P(None, "grid"),
        P("grid"),
        P(None, "grid", None, None),
        P("bundle", "grid", None),
        P("bundle", "grid"),
        P("bundle", "grid", None),
        P("bundle", "grid", None),
        P("bundle", None),
        P(),
    )
    return jax.shard_map(
        shards, mesh=mesh, in_specs=placed, out_specs=P(None, "grid"), check_vma=False
    )
```

```python
import jax
import jax.numpy as jnp
from jax import lax
from jax.experimental import pallas as pl
from jax.experimental.pallas import tpu as pltpu
from jax.sharding import PartitionSpec as P

SUB = 2
NEWTON = 3
SPECIES = 24
CELLS = 4096
SLOTS = 4096
NODES = 2048
LINES = 2
GRID = 128
BUNDLES = 4
CAP = 32
CHUNKS = 64
STEPS = NODES // CHUNKS
TILES = 32
LANES = 128
LOW = 256
HIGH = 16
QUARTER = CELLS // BUNDLES
MESH = pl.DeviceIdType.MESH


def lane_ids(rows):
    return lax.broadcasted_iota(jnp.int32, (rows, LANES), 1)


def row_ids(rows=8):
    return lax.broadcasted_iota(jnp.int32, (rows, LANES), 0)


def swap_blocks(parts):
    lane = lane_ids(parts[0].shape[0])
    far = lane < 64
    near = (lane & 32) == 0
    a, b, c, d = parts
    a, c = jnp.where(far, a, pltpu.roll(c, 64, 1)), jnp.where(far, pltpu.roll(a, 64, 1), c)
    b, d = jnp.where(far, b, pltpu.roll(d, 64, 1)), jnp.where(far, pltpu.roll(b, 64, 1), d)
    a, b = jnp.where(near, a, pltpu.roll(b, 32, 1)), jnp.where(near, pltpu.roll(a, 96, 1), b)
    c, d = jnp.where(near, c, pltpu.roll(d, 32, 1)), jnp.where(near, pltpu.roll(c, 96, 1), d)
    return a, b, c, d


def to_groups(v0, v1, v2):
    row = row_ids()
    last = jnp.where(
        row < 2,
        pltpu.roll(v0, 2, 0),
        jnp.where(row < 4, pltpu.roll(v1, 4, 0), pltpu.roll(v2, 6, 0)),
    )
    return v0, v1, v2, last


def from_groups(g0, g1, g2, g3):
    row = row_ids()
    low = row < 6
    return (
        jnp.where(low, g0, pltpu.roll(g3, 6, 0)),
        jnp.where(low, g1, pltpu.roll(g3, 4, 0)),
        jnp.where(low, g2, pltpu.roll(g3, 2, 0)),
    )


def to_blocks(v0, v1, v2, flux):
    row = row_ids()
    head = row < 5
    return (
        jnp.where(head, v0, pltpu.roll(v2, 5, 0)),
        jnp.where(head, v1, pltpu.roll(v2, 3, 0)),
        jnp.where(
            row < 3,
            pltpu.roll(v0, 3, 0),
            jnp.where(head, pltpu.roll(v1, 6, 0), pltpu.roll(v2, 1, 0)),
        ),
        jnp.where(
            row < 1,
            pltpu.roll(v1, 1, 0),
            jnp.where(head, pltpu.roll(flux, 1, 0), pltpu.roll(v2, 7, 0)),
        ),
    )


def from_first(g0, g1, g2, g3):
    row = row_ids()
    head = row < 5
    return (
        jnp.where(head, g0, pltpu.roll(g2, 5, 0)),
        jnp.where(head, g1, jnp.where(row < 7, pltpu.roll(g2, 2, 0), pltpu.roll(g3, 7, 0))),
        jnp.where(row < 1, pltpu.roll(g3, 7, 0), 0.0),
    )


def from_second(g0, g1, g2, g3):
    row = row_ids()
    return jnp.where(
        row < 4,
        jnp.where(row < 2, g0, pltpu.roll(g1, 2, 0)),
        jnp.where(row < 6, pltpu.roll(g2, 4, 0), pltpu.roll(g3, 6, 0)),
    )


def gather_tile(load, index, count, found):
    lane = jnp.broadcast_to(index & 127, (8, LANES))
    tile = jnp.broadcast_to(index >> 7, (8, LANES))
    for k in range(count):
        here = tile == k
        for g in range(3):
            found[g] = jnp.where(here, jnp.take_along_axis(load(k, g), lane, axis=1), found[g])
    return found


def expand(tiles, indices, highs):
    tops = []
    rests = []
    for tile, index in zip(tiles, indices):
        top = tile.astype(jnp.bfloat16).astype(jnp.float32)
        rest = tile - top
        high = jnp.broadcast_to(index >> 8, tile.shape)
        column = [[], []]
        for k in highs:
            here = high == k
            column[0].append(jnp.where(here, top, 0.0))
            column[1].append(jnp.where(here, rest, 0.0))
        tops.append(jnp.concatenate(column[0], 0).astype(jnp.bfloat16))
        rests.append(jnp.concatenate(column[1], 0).astype(jnp.bfloat16))
    return jnp.concatenate(tops + rests, 1)


def hot_tile(index):
    low = jnp.broadcast_to(index & (LOW - 1), (LOW, LANES))
    hot = lax.broadcasted_iota(jnp.int32, (LOW, LANES), 0) == low
    return hot.astype(jnp.float32).astype(jnp.bfloat16)


def contract(left, hots):
    right = jnp.concatenate(hots + hots, 1)
    return lax.dot_general(
        left, right, (((1,), (1,)), ((), ())), preferred_element_type=jnp.float32
    )


def side_by_side(blocks):
    lane = lane_ids(32)
    out = blocks[0]
    for j in range(1, 4):
        out = jnp.where(lane >= 32 * j, pltpu.roll(blocks[j], 32 * j, 1), out)
    return out


def by_step(source_ref, lines_ref, square_ref):
    for m in range(16):
        lines_ref[2 * m : 2 * m + 2, :] = source_ref[:, m * LANES : (m + 1) * LANES]
    square_ref[:, 0:32] = jnp.transpose(lines_ref[...], (1, 0))
    mixed = side_by_side([square_ref[32 * q : 32 * q + 32, :] for q in range(4)])
    lane = lane_ids(8)
    take = (lane & 3) * 32 + ((lane >> 2) & 15) * 2 + (lane >> 6)
    return jnp.concatenate(
        [jnp.take_along_axis(mixed[8 * j : 8 * j + 8], take, axis=1) for j in range(4)], 0
    )


ORDER = (2, 1, 3, 0)


def kernel(
    cell_hbm,
    pore_hbm,
    request_hbm,
    slot_hbm,
    length_hbm,
    courant_hbm,
    weight_hbm,
    inflow_hbm,
    inter_hbm,
    out_ref,
    cell_ref,
    pore_ref,
    request_in,
    slot_in,
    length_in,
    courant_in,
    weight_in,
    inflow_in,
    inter_in,
    square_i,
    square_f,
    lines_i,
    lines_f,
    request_ref,
    slot_ref,
    weight_ref,
    scale_ref,
    decay_ref,
    span_ref,
    hot_slot,
    hot_request,
    send1,
    recv1,
    send_a,
    recv_a,
    send_b,
    recv_b,
    table,
    state,
    rows,
    acc,
    acc_a,
    acc_b,
    part,
    part_flux,
    got,
    got_flux,
    in_sem,
    own_sem,
    send1_sem,
    recv1_sem,
    send_a_sem,
    recv_a_sem,
    send_b_sem,
    recv_b_sem,
    send3_sem,
    recv3_sem,
    send4_sem,
    recv4_sem,
    send5_sem,
    recv5_sem,
    send6_sem,
    recv6_sem,
    send7_sem,
    recv7_sem,
):
    me = lax.axis_index("grid")
    mine = lax.axis_index("bundle")
    my_y = lax.div(me, 32)
    my_z = lax.rem(lax.div(me, 2), 16)
    my_core = lax.rem(me, 2)

    loads = [
        pltpu.make_async_copy(source, target, in_sem.at[j])
        for j, (source, target) in enumerate(
            (
                (request_hbm.at[mine], request_in),
                (cell_hbm, cell_ref),
                (slot_hbm, slot_in),
                (courant_hbm, courant_in),
                (weight_hbm, weight_in),
                (length_hbm, length_in),
                (inflow_hbm, inflow_in),
                (inter_hbm, inter_in),
                (pore_hbm, pore_ref),
            )
        )
    ]
    for load in loads:
        load.start()

    barrier = pltpu.get_barrier_semaphore()

    def greet(k, _):
        pl.semaphore_signal(
            barrier, inc=1, device_id=(lax.rem(me + k, GRID), mine), device_id_type=MESH
        )
        return 0

    lax.fori_loop(1, GRID, greet, 0)
    for k in range(1, BUNDLES):
        pl.semaphore_signal(
            barrier, inc=1, device_id=(me, lax.rem(mine + k, BUNDLES)), device_id_type=MESH
        )

    loads[0].wait()
    square_i[:, 0:32] = jnp.transpose(request_in[...], (1, 0))
    request_ref[...] = side_by_side([square_i[pl.ds(d, 32, stride=4), :] for d in range(4)])
    loads[1].wait()

    def pick(t, _):
        found = gather_tile(
            lambda k, g: cell_ref[8 * g : 8 * g + 8, k * LANES : (k + 1) * LANES],
            request_ref[pl.ds(t, 1), :],
            TILES,
            [jnp.zeros((8, LANES), jnp.float32)] * 3,
        )
        blocks = swap_blocks(to_groups(*found))
        for d in range(4):
            send1[t * 4 + d] = blocks[d][:6]
        return 0

    def post_one(source, target, send_sem, recv_sem, peer):
        pltpu.make_async_remote_copy(
            src_ref=source.at[peer],
            dst_ref=target.at[me],
            send_sem=send_sem,
            recv_sem=recv_sem,
            device_id=(peer, mine),
            device_id_type=MESH,
        ).start()

    def post(source, target, send_sem, recv_sems, r):
        first = lax.rem(my_y + r, 4) * 32

        def ring(j, _):
            hop = 8 + lax.div(j + 1, 2) * (1 - 2 * lax.rem(j, 2))
            spot = first + lax.rem(my_z + hop, 16) * 2
            for core in range(2):
                post_one(source, target, send_sem, recv_sems.at[r], spot + core)
            return 0

        lax.fori_loop(0, 16 if r else 15, ring, 0)
        if r == 0:
            post_one(
                source, target, send_sem, recv_sems.at[0], first + my_z * 2 + 1 - my_core
            )
            own = pltpu.make_async_copy(source.at[me], target.at[me], own_sem)
            own.start()
            own.wait()

    def arrived(target, recv_sems, r):
        blocks = pl.ds(0, 32 if r else 31)
        pltpu.make_async_copy(target.at[blocks], target.at[blocks], recv_sems.at[r]).wait()
        return lax.rem(my_y + 4 - r, 4)

    def sent(source, send_sem):
        blocks = pl.ds(0, GRID - 1)
        pltpu.make_async_copy(source.at[blocks], source.at[blocks], send_sem).wait()

    for step, r in enumerate(ORDER):
        first = lax.rem(my_y + r, 4) * 8
        lax.fori_loop(0, 8, lambda t, c, first=first: pick(first + t, c), 0, unroll=2)
        if step == 0:
            pl.semaphore_wait(barrier, GRID - 1 + BUNDLES - 1)
        post(send1, recv1, send1_sem, recv1_sem, r)

    for load in loads[2:]:
        load.wait()
    slot_ref[...] = by_step(slot_in, lines_i, square_i)
    courant = by_step(courant_in, lines_f, square_f)
    scale = 1.0 / (1.0 + courant)
    scale_ref[...] = scale
    decay_ref[...] = courant * scale
    span_ref[0:1, :] = decay_ref[0:1, :]
    for i in range(1, STEPS):
        span_ref[i : i + 1, :] = span_ref[i - 1 : i, :] * decay_ref[i : i + 1, :]
    flux = by_step(weight_in, lines_f, square_f)
    lane = lane_ids(32)
    node = (lane & (CHUNKS - 1)) * STEPS + row_ids(32)
    first_line = jnp.broadcast_to(length_in[:, 0:1], (32, LANES))
    second_line = jnp.broadcast_to(length_in[:, 1:2], (32, LANES))
    weight_ref[...] = jnp.where(node < jnp.where(lane < CHUNKS, first_line, second_line), flux, 0.0)

    def heat(t, _):
        hot_slot[t] = hot_tile(slot_ref[pl.ds(t, 1), :])
        hot_request[t] = hot_tile(request_ref[pl.ds(t, 1), :])
        return 0

    lax.fori_loop(0, TILES, heat, 0)
    square = lax.broadcasted_iota(jnp.int32, (SPECIES, SPECIES), 0) == lax.broadcasted_iota(
        jnp.int32, (SPECIES, SPECIES), 1
    )
    entry = jnp.sum(
        jnp.where(square, jnp.broadcast_to(inflow_in[...], (SPECIES, SPECIES)), 0.0),
        axis=1,
        keepdims=True,
    )
    entry = jnp.broadcast_to(entry, (SPECIES, LANES))
    square_f[0:SPECIES, :] = jnp.zeros((SPECIES, LANES), jnp.float32)
    square_f[0:SPECIES, 0:SPECIES] = inter_in[...]
    inter = square_f[0:SPECIES, :]
    inter_top = inter.astype(jnp.bfloat16).astype(jnp.float32)
    inter_rest = inter - inter_top
    inter = inter_top + pltpu.roll(inter_top, 32, 1) + pltpu.roll(inter_rest, 64, 1)
    inter = inter.astype(jnp.bfloat16)
    chunk = lane_ids(SPECIES) & (CHUNKS - 1)
    levels = []
    level = jnp.broadcast_to(span_ref[STEPS - 1 : STEPS, :], (SPECIES, LANES))
    span_all = level
    for bit in range(6):
        levels.append(level)
        behind = pltpu.roll(level, 1 << bit, 1)
        level = jnp.where(chunk >= (1 << bit), level * behind, level)

    for step, r in enumerate(ORDER):
        base = arrived(recv1, recv1_sem, r) * 8
        pad = jnp.zeros((2, LANES), jnp.float32)
        for u in range(8):
            parts = [
                jnp.concatenate([recv1[base * 4 + u * 4 + d], pad], 0) for d in range(4)
            ]
            for g, value in enumerate(from_groups(*swap_blocks(parts))):
                table[u, 8 * g : 8 * g + 8, :] = value

        def fetch(t, _, base=base, step=step):
            if step == 0:
                found = [jnp.zeros((8, LANES), jnp.float32)] * 3
            else:
                found = [state[t, 8 * g : 8 * g + 8, :] for g in range(3)]
            found = gather_tile(
                lambda k, g: table[k, 8 * g : 8 * g + 8, :],
                slot_ref[pl.ds(t, 1), :] - base * LANES,
                8,
                found,
            )
            for g in range(3):
                state[t, 8 * g : 8 * g + 8, :] = found[g]
            return 0

        lax.fori_loop(0, TILES, fetch, 0, unroll=4)

    def row(ref, i):
        return jnp.broadcast_to(ref[i : i + 1, :], (SPECIES, LANES))

    for substep in range(SUB):
        value = jnp.zeros((SPECIES, LANES), jnp.float32)
        for i in range(STEPS):
            value = row(decay_ref, i) * value + row(scale_ref, i) * state[i]
            state[i] = value
        ends = jnp.where(chunk == 0, value + span_all * entry, value)
        for bit in range(6):
            behind = pltpu.roll(ends, 1 << bit, 1)
            ends = jnp.where(chunk >= (1 << bit), ends + levels[bit] * behind, ends)
        before = jnp.where(chunk == 0, entry, pltpu.roll(ends, 1, 1))
        for i in range(STEPS):
            state[i] = state[i] + row(span_ref, i) * before

    def react(j, _):
        base = jnp.concatenate([state[j * 4 + q] for q in range(4)], 1)
        gap = jnp.zeros((8, 4 * LANES), jnp.float32)
        iterate = base
        for _step in range(NEWTON):
            active = jnp.concatenate([jnp.tanh(iterate), gap], 0)
            top = active.astype(jnp.bfloat16)
            rest = (active - top.astype(jnp.float32)).astype(jnp.bfloat16)
            stack = jnp.concatenate([top, rest, top, jnp.zeros_like(top)], 0)
            iterate = base - jnp.dot(inter, stack, preferred_element_type=jnp.float32)
        for q in range(4):
            weight = jnp.broadcast_to(weight_ref[pl.ds(j * 4 + q, 1), :], (8, LANES))
            result = iterate[:, q * LANES : (q + 1) * LANES]
            for g in range(3):
                rows[j * 4 + q, 8 * g : 8 * g + 8, :] = result[8 * g : 8 * g + 8] * weight
            rows[j * 4 + q, 24:32, :] = jnp.where(row_ids() == 0, weight, 0.0)
        return 0

    lax.fori_loop(0, TILES // 4, react, 0, unroll=4)

    sent(send1, send1_sem)
    for half in range(2):
        ys = [lax.rem(my_y + r, 4) for r in ORDER[2 * half : 2 * half + 2]]
        highs = [y * 4 + sub for y in ys for sub in range(4)]
        total = None
        for j in range(TILES // 4):
            span = range(4 * j, 4 * j + 4)
            left = expand([rows[t] for t in span], [slot_ref[t : t + 1, :] for t in span], highs)
            more = contract(left, [hot_slot[t] for t in span])
            if j == 0:
                acc[0:LOW, :] = more
            else:
                acc[0:LOW, :] += more
        for k in range(8):
            for side in range(2):
                lanes = slice(side * LANES, (side + 1) * LANES)
                blocks = swap_blocks(
                    to_blocks(*[acc[k * 32 + 8 * g : k * 32 + 8 * g + 8, lanes] for g in range(4)])
                )
                for d in range(4):
                    send_a[highs[k] * 8 + side * 4 + d] = blocks[d][:5]
                    send_b[highs[k] * 8 + side * 4 + d] = blocks[d][5:7]
        for r in ORDER[2 * half : 2 * half + 2]:
            post(send_a, recv_a, send_a_sem, recv_a_sem, r)
    for r in ORDER:
        post(send_b, recv_b, send_b_sem, recv_b_sem, r)

    def collect(target, recv_sems, step, pad_rows, combine, total):
        base = arrived(target, recv_sems, ORDER[step]) * 8
        pad = jnp.zeros((pad_rows, LANES), jnp.float32)
        indices = request_ref[pl.ds(pl.multiple_of(base, 8), 8), :]
        for j in range(2):
            span = range(4 * j, 4 * j + 4)
            tiles = []
            for u in span:
                parts = [
                    jnp.concatenate([target[base * 4 + u * 4 + d], pad], 0) for d in range(4)
                ]
                tiles.append(combine(*swap_blocks(parts)))
            left = expand(tiles, [indices[u : u + 1] for u in span], range(HIGH))
            more = contract(left, [hot_request[base + u] for u in span])
            if step == 0 and j == 0:
                total[...] = more
            else:
                total[...] += more

    def over_bundles(pairs):
        copies = []
        for k in (2, 1, 3):
            peer = lax.rem(mine + k, BUNDLES)
            cells = pl.ds(pl.multiple_of(peer * QUARTER, QUARTER), QUARTER)
            for source, target, sends, recvs in pairs:
                copy = pltpu.make_async_remote_copy(
                    src_ref=source(cells),
                    dst_ref=target(k - 1),
                    send_sem=sends.at[k - 1],
                    recv_sem=recvs.at[k - 1],
                    device_id=(me, peer),
                    device_id_type=MESH,
                )
                copy.start()
                copies.append(copy)
        return copies

    ours = pl.ds(pl.multiple_of(mine * QUARTER, QUARTER), QUARTER)

    def finish(species, sends, recvs):
        total = part[species, ours] + got[0, species] + got[1, species] + got[2, species]
        flux = part_flux[:, ours] + got_flux[0] + got_flux[1] + got_flux[2]
        pore = pore_ref[:, ours]
        out_ref[species, ours] = (pore * cell_ref[species, ours] + total) / (pore + flux)
        return over_bundles(
            [
                (
                    lambda cells: out_ref.at[species, ours],
                    lambda k: out_ref.at[species, ours],
                    sends,
                    recvs,
                )
            ]
        )

    first = slice(0, 16)
    second = slice(16, 24)
    for step in range(4):
        collect(
            recv_a, recv_a_sem, step, 3, lambda *g: jnp.concatenate(from_first(*g), 0), acc_a
        )
    for h in range(HIGH):
        for side in range(2):
            lanes = slice(side * LANES, (side + 1) * LANES)
            cells = slice((h * 2 + side) * LANES, (h * 2 + side + 1) * LANES)
            part[0:16, cells] = acc_a[h * 24 : h * 24 + 16, lanes]
            part_flux[:, cells] = acc_a[h * 24 + 16 : h * 24 + 17, lanes]
    sums_first = over_bundles(
        [
            (lambda cells: part.at[first, cells], lambda k: got.at[k, first], send3_sem, recv3_sem),
            (lambda cells: part_flux.at[:, cells], lambda k: got_flux.at[k], send4_sem, recv4_sem),
        ]
    )

    for step in range(4):
        collect(recv_b, recv_b_sem, step, 6, from_second, acc_b)
    for h in range(HIGH):
        for side in range(2):
            cells = slice((h * 2 + side) * LANES, (h * 2 + side + 1) * LANES)
            part[second, cells] = acc_b[h * 8 : h * 8 + 8, side * LANES : (side + 1) * LANES]
    sums_second = over_bundles(
        [(lambda cells: part.at[second, cells], lambda k: got.at[k, second], send6_sem, recv6_sem)]
    )

    for copy in sums_first:
        copy.wait()
    done = finish(first, send5_sem, recv5_sem)
    for copy in sums_second:
        copy.wait()
    done = done + finish(second, send7_sem, recv7_sem)
    sent(send_a, send_a_sem)
    sent(send_b, send_b_sem)
    for copy in done:
        copy.wait()


def shards(
    cell_state,
    pore_volume,
    request_cell,
    node_slot,
    line_length,
    courant,
    flux_weight,
    inflow,
    interaction,
):
    f32 = jnp.float32
    i32 = jnp.int32
    vmem = pltpu.VMEM
    dma = pltpu.SemaphoreType.DMA
    return pl.pallas_call(
        kernel,
        out_shape=jax.ShapeDtypeStruct((SPECIES, CELLS), f32),
        in_specs=[pl.BlockSpec(memory_space=pl.ANY)] * 9,
        out_specs=pl.BlockSpec(memory_space=pltpu.VMEM),
        scratch_shapes=[
            vmem((SPECIES, CELLS), f32),
            vmem((1, CELLS), f32),
            vmem((CAP, GRID), i32),
            vmem((LINES, NODES), i32),
            vmem((1, LINES), i32),
            vmem((LINES, NODES), f32),
            vmem((LINES, NODES), f32),
            vmem((1, SPECIES), f32),
            vmem((SPECIES, SPECIES), f32),
            vmem((LANES, LANES), i32),
            vmem((LANES, LANES), f32),
            vmem((32, LANES), i32),
            vmem((32, LANES), f32),
            vmem((32, LANES), i32),
            vmem((32, LANES), i32),
            vmem((32, LANES), f32),
            vmem((32, LANES), f32),
            vmem((32, LANES), f32),
            vmem((32, LANES), f32),
            vmem((TILES, LOW, LANES), jnp.bfloat16),
            vmem((TILES, LOW, LANES), jnp.bfloat16),
            vmem((GRID, 6, LANES), f32),
            vmem((GRID, 6, LANES), f32),
            vmem((GRID, 5, LANES), f32),
            vmem((GRID, 5, LANES), f32),
            vmem((GRID, 2, LANES), f32),
            vmem((GRID, 2, LANES), f32),
            vmem((8, SPECIES, LANES), f32),
            vmem((TILES, SPECIES, LANES), f32),
            vmem((TILES, 32, LANES), f32),
            vmem((LOW, LOW), f32),
            vmem((HIGH * 24, LOW), f32),
            vmem((HIGH * 8, LOW), f32),
            vmem((SPECIES, CELLS), f32),
            vmem((1, CELLS), f32),
            vmem((BUNDLES - 1, SPECIES, QUARTER), f32),
            vmem((BUNDLES - 1, 1, QUARTER), f32),
            dma((9,)),
            dma,
            dma,
            dma((4,)),
            dma,
            dma((4,)),
            dma,
            dma((4,)),
            dma((3,)),
            dma((3,)),
            dma((3,)),
            dma((3,)),
            dma((3,)),
            dma((3,)),
            dma((3,)),
            dma((3,)),
            dma((3,)),
            dma((3,)),
        ],
        compiler_params=pltpu.CompilerParams(collective_id=0, has_side_effects=True),
        name="streamlines",
    )(
        cell_state,
        pore_volume.reshape(1, CELLS),
        jnp.transpose(request_cell[:, 0], (0, 2, 1)),
        node_slot[0],
        line_length,
        courant[0],
        flux_weight[0],
        inflow,
        interaction,
    )


def solution(mesh):
    placed = (
        P(None, "grid"),
        P("grid"),
        P(None, "grid", None, None),
        P("bundle", "grid", None),
        P("bundle", "grid"),
        P("bundle", "grid", None),
        P("bundle", "grid", None),
        P("bundle", None),
        P(),
    )
    return jax.shard_map(
        shards, mesh=mesh, in_specs=placed, out_specs=P(None, "grid"), check_vma=False
    )
```

```python
import jax
import jax.numpy as jnp
from jax import lax
from jax.experimental import pallas as pl
from jax.experimental.pallas import tpu as pltpu
from jax.sharding import PartitionSpec as P

SUB = 2
NEWTON = 3
SPECIES = 24
CELLS = 4096
SLOTS = 4096
NODES = 2048
LINES = 2
GRID = 128
BUNDLES = 4
CAP = 32
CHUNKS = 64
STEPS = NODES // CHUNKS
TILES = 32
LANES = 128
LOW = 256
HIGH = 16
QUARTER = CELLS // BUNDLES
MESH = pl.DeviceIdType.MESH


def lane_ids(rows):
    return lax.broadcasted_iota(jnp.int32, (rows, LANES), 1)


def row_ids(rows=8):
    return lax.broadcasted_iota(jnp.int32, (rows, LANES), 0)


def swap_blocks(parts):
    lane = lane_ids(parts[0].shape[0])
    far = lane < 64
    near = (lane & 32) == 0
    a, b, c, d = parts
    a, c = jnp.where(far, a, pltpu.roll(c, 64, 1)), jnp.where(far, pltpu.roll(a, 64, 1), c)
    b, d = jnp.where(far, b, pltpu.roll(d, 64, 1)), jnp.where(far, pltpu.roll(b, 64, 1), d)
    a, b = jnp.where(near, a, pltpu.roll(b, 32, 1)), jnp.where(near, pltpu.roll(a, 96, 1), b)
    c, d = jnp.where(near, c, pltpu.roll(d, 32, 1)), jnp.where(near, pltpu.roll(c, 96, 1), d)
    return a, b, c, d


def to_groups(v0, v1, v2):
    row = row_ids()
    last = jnp.where(
        row < 2,
        pltpu.roll(v0, 2, 0),
        jnp.where(row < 4, pltpu.roll(v1, 4, 0), pltpu.roll(v2, 6, 0)),
    )
    return v0, v1, v2, last


def from_groups(g0, g1, g2, g3):
    row = row_ids()
    low = row < 6
    return (
        jnp.where(low, g0, pltpu.roll(g3, 6, 0)),
        jnp.where(low, g1, pltpu.roll(g3, 4, 0)),
        jnp.where(low, g2, pltpu.roll(g3, 2, 0)),
    )


def to_blocks(v0, v1, v2, flux):
    row = row_ids()
    head = row < 5
    return (
        jnp.where(head, v0, pltpu.roll(v2, 5, 0)),
        jnp.where(head, v1, pltpu.roll(v2, 3, 0)),
        jnp.where(
            row < 3,
            pltpu.roll(v0, 3, 0),
            jnp.where(head, pltpu.roll(v1, 6, 0), pltpu.roll(v2, 1, 0)),
        ),
        jnp.where(
            row < 1,
            pltpu.roll(v1, 1, 0),
            jnp.where(head, pltpu.roll(flux, 1, 0), pltpu.roll(v2, 7, 0)),
        ),
    )


def from_first(g0, g1, g2, g3):
    row = row_ids()
    head = row < 5
    return (
        jnp.where(head, g0, pltpu.roll(g2, 5, 0)),
        jnp.where(head, g1, jnp.where(row < 7, pltpu.roll(g2, 2, 0), pltpu.roll(g3, 7, 0))),
        jnp.where(row < 1, pltpu.roll(g3, 7, 0), 0.0),
    )


def from_second(g0, g1, g2, g3):
    row = row_ids()
    return jnp.where(
        row < 4,
        jnp.where(row < 2, g0, pltpu.roll(g1, 2, 0)),
        jnp.where(row < 6, pltpu.roll(g2, 4, 0), pltpu.roll(g3, 6, 0)),
    )


def gather_tile(load, index, tiles, found):
    lane = jnp.broadcast_to(index & 127, (8, LANES))
    tile = jnp.broadcast_to(index >> 7, (8, LANES))
    for k, name in enumerate(tiles):
        here = tile == name
        for g in range(3):
            found[g] = jnp.where(here, jnp.take_along_axis(load(k, g), lane, axis=1), found[g])
    return found


def expand(tiles, indices, highs):
    tops = []
    rests = []
    for tile, index in zip(tiles, indices):
        top = tile.astype(jnp.bfloat16).astype(jnp.float32)
        rest = tile - top
        high = jnp.broadcast_to(index >> 8, tile.shape)
        column = [[], []]
        for k in highs:
            here = high == k
            column[0].append(jnp.where(here, top, 0.0))
            column[1].append(jnp.where(here, rest, 0.0))
        tops.append(jnp.concatenate(column[0], 0).astype(jnp.bfloat16))
        rests.append(jnp.concatenate(column[1], 0).astype(jnp.bfloat16))
    return jnp.concatenate(tops + rests, 1)


def hot_tile(index):
    low = jnp.broadcast_to(index & (LOW - 1), (LOW, LANES))
    hot = lax.broadcasted_iota(jnp.int32, (LOW, LANES), 0) == low
    return hot.astype(jnp.float32).astype(jnp.bfloat16)


def contract(left, hots):
    right = jnp.concatenate(hots + hots, 1)
    return lax.dot_general(
        left, right, (((1,), (1,)), ((), ())), preferred_element_type=jnp.float32
    )


def side_by_side(blocks):
    lane = lane_ids(32)
    out = blocks[0]
    for j in range(1, 4):
        out = jnp.where(lane >= 32 * j, pltpu.roll(blocks[j], 32 * j, 1), out)
    return out


def by_step(source_ref, lines_ref, square_ref):
    for m in range(16):
        lines_ref[2 * m : 2 * m + 2, :] = source_ref[:, m * LANES : (m + 1) * LANES]
    square_ref[:, 0:32] = jnp.transpose(lines_ref[...], (1, 0))
    mixed = side_by_side([square_ref[32 * q : 32 * q + 32, :] for q in range(4)])
    lane = lane_ids(8)
    take = (lane & 3) * 32 + ((lane >> 2) & 15) * 2 + (lane >> 6)
    return jnp.concatenate(
        [jnp.take_along_axis(mixed[8 * j : 8 * j + 8], take, axis=1) for j in range(4)], 0
    )


GROUPS = ((2, 0, 4), (2, 4, 8), (1, 0, 8), (3, 0, 8), (0, 0, 4), (0, 4, 8))
SPLITS = ((2,), (1,), (3, 0))


def kernel(
    cell_hbm,
    pore_hbm,
    request_hbm,
    slot_hbm,
    length_hbm,
    courant_hbm,
    weight_hbm,
    inflow_hbm,
    inter_hbm,
    out_ref,
    cell_ref,
    pore_ref,
    request_in,
    slot_in,
    length_in,
    courant_in,
    weight_in,
    inflow_in,
    inter_in,
    square_i,
    square_f,
    lines_i,
    lines_f,
    request_ref,
    slot_ref,
    weight_ref,
    scale_ref,
    decay_ref,
    span_ref,
    hot_slot,
    hot_request,
    send1,
    recv1,
    send_a,
    recv_a,
    send_b,
    recv_b,
    table,
    state,
    rows,
    acc,
    acc_a,
    acc_b,
    part,
    part_flux,
    got,
    got_flux,
    in_sem,
    own_sem,
    send1_sem,
    recv1_sem,
    send_a_sem,
    recv_a_sem,
    send_b_sem,
    recv_b_sem,
    send3_sem,
    recv3_sem,
    send4_sem,
    recv4_sem,
    send5_sem,
    recv5_sem,
    send6_sem,
    recv6_sem,
    send7_sem,
    recv7_sem,
):
    me = lax.axis_index("grid")
    mine = lax.axis_index("bundle")
    my_y = lax.div(me, 32)
    my_pair = lax.rem(lax.div(me, 4), 8)
    my_seat = lax.rem(me, 4)

    loads = [
        pltpu.make_async_copy(source, target, in_sem.at[j])
        for j, (source, target) in enumerate(
            (
                (request_hbm.at[mine], request_in),
                (cell_hbm, cell_ref),
                (slot_hbm, slot_in),
                (courant_hbm, courant_in),
                (weight_hbm, weight_in),
                (length_hbm, length_in),
                (inflow_hbm, inflow_in),
                (inter_hbm, inter_in),
                (pore_hbm, pore_ref),
            )
        )
    ]
    for load in loads:
        load.start()

    barrier = pltpu.get_barrier_semaphore()

    def greet(k, _):
        pl.semaphore_signal(
            barrier, inc=1, device_id=(lax.rem(me + k, GRID), mine), device_id_type=MESH
        )
        return 0

    lax.fori_loop(1, GRID, greet, 0)
    for k in range(1, BUNDLES):
        pl.semaphore_signal(
            barrier, inc=1, device_id=(me, lax.rem(mine + k, BUNDLES)), device_id_type=MESH
        )

    loads[0].wait()
    square_i[:, 0:32] = jnp.transpose(request_in[...], (1, 0))
    request_ref[...] = side_by_side([square_i[pl.ds(d, 32, stride=4), :] for d in range(4)])
    loads[1].wait()

    def pick(t, _):
        found = gather_tile(
            lambda k, g: cell_ref[8 * g : 8 * g + 8, k * LANES : (k + 1) * LANES],
            request_ref[pl.ds(t, 1), :],
            range(TILES),
            [jnp.zeros((8, LANES), jnp.float32)] * 3,
        )
        blocks = swap_blocks(to_groups(*found))
        for d in range(4):
            send1[t * 4 + d] = blocks[d][:6]
        return 0

    def post_one(source, target, send_sem, recv_sem, peer):
        pltpu.make_async_remote_copy(
            src_ref=source.at[peer],
            dst_ref=target.at[me],
            send_sem=send_sem,
            recv_sem=recv_sem,
            device_id=(peer, mine),
            device_id_type=MESH,
        ).start()

    def hop(j):
        return 4 + lax.div(j + 1, 2) * (1 - 2 * lax.rem(j, 2))

    def tile_to(r, j):
        return lax.rem(my_y + r, 4) * 8 + lax.rem(my_pair + hop(j), 8)

    def tile_from(r, j):
        return lax.rem(my_y + 4 - r, 4) * 8 + lax.rem(my_pair + 8 - hop(j), 8)

    def post(source, target, send_sem, recv_sems, group):
        r, low, high = GROUPS[group]
        here = r == 0 and high == 8

        def ring(j, _):
            for seat in range(4):
                post_one(source, target, send_sem, recv_sems.at[group], tile_to(r, j) * 4 + seat)
            return 0

        lax.fori_loop(low, high - here, ring, 0)
        if here:
            for seat in range(1, 4):
                peer = tile_to(0, 7) * 4 + lax.rem(my_seat + seat, 4)
                post_one(source, target, send_sem, recv_sems.at[group], peer)
            own = pltpu.make_async_copy(source.at[me], target.at[me], own_sem)
            own.start()
            own.wait()

    def arrived(target, recv_sems, group):
        r, low, high = GROUPS[group]
        blocks = pl.ds(0, 4 * (high - low) - (r == 0 and high == 8))
        pltpu.make_async_copy(target.at[blocks], target.at[blocks], recv_sems.at[group]).wait()
        return [tile_from(r, j) for j in range(low, high)]

    def sent(source, send_sem):
        blocks = pl.ds(0, GRID - 1)
        pltpu.make_async_copy(source.at[blocks], source.at[blocks], send_sem).wait()

    for group in range(len(GROUPS)):
        r, low, high = GROUPS[group]
        lax.fori_loop(low, high, lambda j, c, r=r: pick(tile_to(r, j), c), 0, unroll=2)
        if group == 0:
            pl.semaphore_wait(barrier, GRID - 1 + BUNDLES - 1)
        post(send1, recv1, send1_sem, recv1_sem, group)

    for load in loads[2:]:
        load.wait()
    slot_ref[...] = by_step(slot_in, lines_i, square_i)
    courant = by_step(courant_in, lines_f, square_f)
    scale = 1.0 / (1.0 + courant)
    scale_ref[...] = scale
    decay_ref[...] = courant * scale
    span_ref[0:1, :] = decay_ref[0:1, :]
    for i in range(1, STEPS):
        span_ref[i : i + 1, :] = span_ref[i - 1 : i, :] * decay_ref[i : i + 1, :]
    flux = by_step(weight_in, lines_f, square_f)
    lane = lane_ids(32)
    node = (lane & (CHUNKS - 1)) * STEPS + row_ids(32)
    first_line = jnp.broadcast_to(length_in[:, 0:1], (32, LANES))
    second_line = jnp.broadcast_to(length_in[:, 1:2], (32, LANES))
    weight_ref[...] = jnp.where(node < jnp.where(lane < CHUNKS, first_line, second_line), flux, 0.0)

    def heat(t, _):
        hot_slot[t] = hot_tile(slot_ref[pl.ds(t, 1), :])
        hot_request[t] = hot_tile(request_ref[pl.ds(t, 1), :])
        return 0

    lax.fori_loop(0, TILES, heat, 0)
    square = lax.broadcasted_iota(jnp.int32, (SPECIES, SPECIES), 0) == lax.broadcasted_iota(
        jnp.int32, (SPECIES, SPECIES), 1
    )
    entry = jnp.sum(
        jnp.where(square, jnp.broadcast_to(inflow_in[...], (SPECIES, SPECIES)), 0.0),
        axis=1,
        keepdims=True,
    )
    entry = jnp.broadcast_to(entry, (SPECIES, LANES))
    square_f[0:SPECIES, :] = jnp.zeros((SPECIES, LANES), jnp.float32)
    square_f[0:SPECIES, 0:SPECIES] = inter_in[...]
    inter = square_f[0:SPECIES, :]
    inter_top = inter.astype(jnp.bfloat16).astype(jnp.float32)
    inter_rest = inter - inter_top
    inter = inter_top + pltpu.roll(inter_top, 32, 1) + pltpu.roll(inter_rest, 64, 1)
    inter = inter.astype(jnp.bfloat16)
    chunk = lane_ids(SPECIES) & (CHUNKS - 1)
    levels = []
    level = jnp.broadcast_to(span_ref[STEPS - 1 : STEPS, :], (SPECIES, LANES))
    span_all = level
    for bit in range(6):
        levels.append(level)
        behind = pltpu.roll(level, 1 << bit, 1)
        level = jnp.where(chunk >= (1 << bit), level * behind, level)

    for group in range(len(GROUPS)):
        names = arrived(recv1, recv1_sem, group)
        pad = jnp.zeros((2, LANES), jnp.float32)
        for u, name in enumerate(names):
            parts = [jnp.concatenate([recv1[name * 4 + d], pad], 0) for d in range(4)]
            for g, value in enumerate(from_groups(*swap_blocks(parts))):
                table[u, 8 * g : 8 * g + 8, :] = value

        def fetch(t, _, names=names, group=group):
            if group == 0:
                found = [jnp.zeros((8, LANES), jnp.float32)] * 3
            else:
                found = [state[t, 8 * g : 8 * g + 8, :] for g in range(3)]
            found = gather_tile(
                lambda k, g: table[k, 8 * g : 8 * g + 8, :],
                slot_ref[pl.ds(t, 1), :],
                names,
                found,
            )
            for g in range(3):
                state[t, 8 * g : 8 * g + 8, :] = found[g]
            return 0

        lax.fori_loop(0, TILES, fetch, 0, unroll=4)

    def row(ref, i):
        return jnp.broadcast_to(ref[i : i + 1, :], (SPECIES, LANES))

    before = None
    for substep in range(SUB):
        value = jnp.zeros((SPECIES, LANES), jnp.float32)
        for i in range(STEPS):
            held = state[i]
            if substep > 0:
                held = held + row(span_ref, i) * before
            value = row(decay_ref, i) * value + row(scale_ref, i) * held
            state[i] = value
        ends = jnp.where(chunk == 0, value + span_all * entry, value)
        for bit in range(6):
            behind = pltpu.roll(ends, 1 << bit, 1)
            ends = jnp.where(chunk >= (1 << bit), ends + levels[bit] * behind, ends)
        before = jnp.where(chunk == 0, entry, pltpu.roll(ends, 1, 1))

    def react(j, _):
        base = jnp.concatenate(
            [
                state[j * 4 + q]
                + jnp.broadcast_to(span_ref[pl.ds(j * 4 + q, 1), :], (SPECIES, LANES)) * before
                for q in range(4)
            ],
            1,
        )
        gap = jnp.zeros((8, 4 * LANES), jnp.float32)
        iterate = base
        for _step in range(NEWTON):
            active = jnp.concatenate([jnp.tanh(iterate), gap], 0)
            top = active.astype(jnp.bfloat16)
            rest = (active - top.astype(jnp.float32)).astype(jnp.bfloat16)
            stack = jnp.concatenate([top, rest, top, jnp.zeros_like(top)], 0)
            iterate = base - jnp.dot(inter, stack, preferred_element_type=jnp.float32)
        for q in range(4):
            weight = jnp.broadcast_to(weight_ref[pl.ds(j * 4 + q, 1), :], (8, LANES))
            result = iterate[:, q * LANES : (q + 1) * LANES]
            for g in range(3):
                rows[j * 4 + q, 8 * g : 8 * g + 8, :] = result[8 * g : 8 * g + 8] * weight
            rows[j * 4 + q, 24:32, :] = jnp.where(row_ids() == 0, weight, 0.0)
        return 0

    lax.fori_loop(0, TILES // 4, react, 0, unroll=4)

    sent(send1, send1_sem)
    for split in SPLITS:
        ys = [lax.rem(my_y + r, 4) for r in split]
        height = 128 * len(split)
        highs = [y * 4 + sub for y in ys for sub in range(4)]
        for j in range(TILES // 4):
            span = range(4 * j, 4 * j + 4)
            left = expand([rows[t] for t in span], [slot_ref[t : t + 1, :] for t in span], highs)
            more = contract(left, [hot_slot[t] for t in span])
            if j == 0:
                acc[0:height, :] = more
            else:
                acc[0:height, :] += more
        for k in range(len(highs)):
            for side in range(2):
                lanes = slice(side * LANES, (side + 1) * LANES)
                blocks = swap_blocks(
                    to_blocks(*[acc[k * 32 + 8 * g : k * 32 + 8 * g + 8, lanes] for g in range(4)])
                )
                for d in range(4):
                    send_a[highs[k] * 8 + side * 4 + d] = blocks[d][:5]
                    send_b[highs[k] * 8 + side * 4 + d] = blocks[d][5:7]
        for group in range(len(GROUPS)):
            if GROUPS[group][0] in split:
                post(send_a, recv_a, send_a_sem, recv_a_sem, group)
    for group in range(len(GROUPS)):
        post(send_b, recv_b, send_b_sem, recv_b_sem, group)

    def collect(target, recv_sems, group, pad_rows, combine, total):
        names = arrived(target, recv_sems, group)
        pad = jnp.zeros((pad_rows, LANES), jnp.float32)
        for j in range(0, len(names), 4):
            span = names[j : j + 4]
            tiles = []
            for name in span:
                parts = [jnp.concatenate([target[name * 4 + d], pad], 0) for d in range(4)]
                tiles.append(combine(*swap_blocks(parts)))
            left = expand(tiles, [request_ref[pl.ds(name, 1), :] for name in span], range(HIGH))
            more = contract(left, [hot_request[name] for name in span])
            if group == 0 and j == 0:
                total[...] = more
            else:
                total[...] += more

    def over_bundles(pairs):
        copies = []
        for k in (2, 1, 3):
            peer = lax.rem(mine + k, BUNDLES)
            cells = pl.ds(pl.multiple_of(peer * QUARTER, QUARTER), QUARTER)
            for source, target, sends, recvs in pairs:
                copy = pltpu.make_async_remote_copy(
                    src_ref=source(cells),
                    dst_ref=target(k - 1),
                    send_sem=sends.at[k - 1],
                    recv_sem=recvs.at[k - 1],
                    device_id=(me, peer),
                    device_id_type=MESH,
                )
                copy.start()
                copies.append(copy)
        return copies

    ours = pl.ds(pl.multiple_of(mine * QUARTER, QUARTER), QUARTER)

    def finish(species, sends, recvs):
        total = part[species, ours] + got[0, species] + got[1, species] + got[2, species]
        flux = part_flux[:, ours] + got_flux[0] + got_flux[1] + got_flux[2]
        pore = pore_ref[:, ours]
        out_ref[species, ours] = (pore * cell_ref[species, ours] + total) / (pore + flux)
        return over_bundles(
            [
                (
                    lambda cells: out_ref.at[species, ours],
                    lambda k: out_ref.at[species, ours],
                    sends,
                    recvs,
                )
            ]
        )

    first = slice(0, 16)
    second = slice(16, 24)
    for group in range(len(GROUPS)):
        collect(
            recv_a, recv_a_sem, group, 3, lambda *g: jnp.concatenate(from_first(*g), 0), acc_a
        )
    for h in range(HIGH):
        for side in range(2):
            lanes = slice(side * LANES, (side + 1) * LANES)
            cells = slice((h * 2 + side) * LANES, (h * 2 + side + 1) * LANES)
            part[0:16, cells] = acc_a[h * 24 : h * 24 + 16, lanes]
            part_flux[:, cells] = acc_a[h * 24 + 16 : h * 24 + 17, lanes]
    sums_first = over_bundles(
        [
            (lambda cells: part.at[first, cells], lambda k: got.at[k, first], send3_sem, recv3_sem),
            (lambda cells: part_flux.at[:, cells], lambda k: got_flux.at[k], send4_sem, recv4_sem),
        ]
    )

    for group in range(len(GROUPS)):
        collect(recv_b, recv_b_sem, group, 6, from_second, acc_b)
    for h in range(HIGH):
        for side in range(2):
            cells = slice((h * 2 + side) * LANES, (h * 2 + side + 1) * LANES)
            part[second, cells] = acc_b[h * 8 : h * 8 + 8, side * LANES : (side + 1) * LANES]
    sums_second = over_bundles(
        [(lambda cells: part.at[second, cells], lambda k: got.at[k, second], send6_sem, recv6_sem)]
    )

    for copy in sums_first:
        copy.wait()
    done = finish(first, send5_sem, recv5_sem)
    for copy in sums_second:
        copy.wait()
    done = done + finish(second, send7_sem, recv7_sem)
    sent(send_a, send_a_sem)
    sent(send_b, send_b_sem)
    for copy in done:
        copy.wait()


def shards(
    cell_state,
    pore_volume,
    request_cell,
    node_slot,
    line_length,
    courant,
    flux_weight,
    inflow,
    interaction,
):
    f32 = jnp.float32
    i32 = jnp.int32
    vmem = pltpu.VMEM
    dma = pltpu.SemaphoreType.DMA
    return pl.pallas_call(
        kernel,
        out_shape=jax.ShapeDtypeStruct((SPECIES, CELLS), f32),
        in_specs=[pl.BlockSpec(memory_space=pltpu.HBM)] * 9,
        out_specs=pl.BlockSpec(memory_space=pltpu.VMEM),
        scratch_shapes=[
            vmem((SPECIES, CELLS), f32),
            vmem((1, CELLS), f32),
            vmem((CAP, GRID), i32),
            vmem((LINES, NODES), i32),
            vmem((1, LINES), i32),
            vmem((LINES, NODES), f32),
            vmem((LINES, NODES), f32),
            vmem((1, SPECIES), f32),
            vmem((SPECIES, SPECIES), f32),
            vmem((LANES, LANES), i32),
            vmem((LANES, LANES), f32),
            vmem((32, LANES), i32),
            vmem((32, LANES), f32),
            vmem((32, LANES), i32),
            vmem((32, LANES), i32),
            vmem((32, LANES), f32),
            vmem((32, LANES), f32),
            vmem((32, LANES), f32),
            vmem((32, LANES), f32),
            vmem((TILES, LOW, LANES), jnp.bfloat16),
            vmem((TILES, LOW, LANES), jnp.bfloat16),
            vmem((GRID, 6, LANES), f32),
            vmem((GRID, 6, LANES), f32),
            vmem((GRID, 5, LANES), f32),
            vmem((GRID, 5, LANES), f32),
            vmem((GRID, 2, LANES), f32),
            vmem((GRID, 2, LANES), f32),
            vmem((8, SPECIES, LANES), f32),
            vmem((TILES, SPECIES, LANES), f32),
            vmem((TILES, 32, LANES), f32),
            vmem((LOW, LOW), f32),
            vmem((HIGH * 24, LOW), f32),
            vmem((HIGH * 8, LOW), f32),
            vmem((SPECIES, CELLS), f32),
            vmem((1, CELLS), f32),
            vmem((BUNDLES - 1, SPECIES, QUARTER), f32),
            vmem((BUNDLES - 1, 1, QUARTER), f32),
            dma((9,)),
            dma,
            dma,
            dma((len(GROUPS),)),
            dma,
            dma((len(GROUPS),)),
            dma,
            dma((len(GROUPS),)),
            dma((3,)),
            dma((3,)),
            dma((3,)),
            dma((3,)),
            dma((3,)),
            dma((3,)),
            dma((3,)),
            dma((3,)),
            dma((3,)),
            dma((3,)),
        ],
        compiler_params=pltpu.CompilerParams(
            collective_id=0, has_side_effects=True, vmem_limit_bytes=20 << 20
        ),
        name="streamlines",
    )(
        *[
            pltpu.with_memory_space_constraint(x, pltpu.HBM)
            for x in (
                cell_state,
                pore_volume.reshape(1, CELLS),
                jnp.transpose(request_cell[:, 0], (0, 2, 1)),
                node_slot[0],
                line_length,
                courant[0],
                flux_weight[0],
                inflow,
                interaction,
            )
        ]
    )


def solution(mesh):
    placed = (
        P(None, "grid"),
        P("grid"),
        P(None, "grid", None, None),
        P("bundle", "grid", None),
        P("bundle", "grid"),
        P("bundle", "grid", None),
        P("bundle", "grid", None),
        P("bundle", None),
        P(),
    )
    return jax.shard_map(
        shards, mesh=mesh, in_specs=placed, out_specs=P(None, "grid"), check_vma=False
    )
```

```python
import jax
import jax.numpy as jnp
from jax import lax
from jax.experimental import pallas as pl
from jax.experimental.pallas import tpu as pltpu
from jax.sharding import PartitionSpec as P

SUB = 2
NEWTON = 3
SPECIES = 24
CELLS = 4096
SLOTS = 4096
NODES = 2048
LINES = 2
GRID = 128
BUNDLES = 4
CAP = 32
CHUNKS = 64
STEPS = NODES // CHUNKS
TILES = 32
LANES = 128
LOW = 256
HIGH = 16
QUARTER = CELLS // BUNDLES
MESH = pl.DeviceIdType.MESH


def lane_ids(rows):
    return lax.broadcasted_iota(jnp.int32, (rows, LANES), 1)


def row_ids(rows=8):
    return lax.broadcasted_iota(jnp.int32, (rows, LANES), 0)


def swap_blocks(parts):
    lane = lane_ids(parts[0].shape[0])
    far = lane < 64
    near = (lane & 32) == 0
    a, b, c, d = parts
    a, c = jnp.where(far, a, pltpu.roll(c, 64, 1)), jnp.where(far, pltpu.roll(a, 64, 1), c)
    b, d = jnp.where(far, b, pltpu.roll(d, 64, 1)), jnp.where(far, pltpu.roll(b, 64, 1), d)
    a, b = jnp.where(near, a, pltpu.roll(b, 32, 1)), jnp.where(near, pltpu.roll(a, 96, 1), b)
    c, d = jnp.where(near, c, pltpu.roll(d, 32, 1)), jnp.where(near, pltpu.roll(c, 96, 1), d)
    return a, b, c, d


def to_groups(v0, v1, v2):
    row = row_ids()
    last = jnp.where(
        row < 2,
        pltpu.roll(v0, 2, 0),
        jnp.where(row < 4, pltpu.roll(v1, 4, 0), pltpu.roll(v2, 6, 0)),
    )
    return v0, v1, v2, last


def from_groups(g0, g1, g2, g3):
    row = row_ids()
    low = row < 6
    return (
        jnp.where(low, g0, pltpu.roll(g3, 6, 0)),
        jnp.where(low, g1, pltpu.roll(g3, 4, 0)),
        jnp.where(low, g2, pltpu.roll(g3, 2, 0)),
    )


def to_blocks(v0, v1, v2, flux):
    row = row_ids()
    head = row < 5
    return (
        jnp.where(head, v0, pltpu.roll(v2, 5, 0)),
        jnp.where(head, v1, pltpu.roll(v2, 3, 0)),
        jnp.where(
            row < 3,
            pltpu.roll(v0, 3, 0),
            jnp.where(head, pltpu.roll(v1, 6, 0), pltpu.roll(v2, 1, 0)),
        ),
        jnp.where(
            row < 1,
            pltpu.roll(v1, 1, 0),
            jnp.where(head, pltpu.roll(flux, 1, 0), pltpu.roll(v2, 7, 0)),
        ),
    )


def from_first(g0, g1, g2, g3):
    row = row_ids()
    head = row < 5
    return (
        jnp.where(head, g0, pltpu.roll(g2, 5, 0)),
        jnp.where(head, g1, jnp.where(row < 7, pltpu.roll(g2, 2, 0), pltpu.roll(g3, 7, 0))),
        jnp.where(row < 1, pltpu.roll(g3, 7, 0), 0.0),
    )


def from_second(g0, g1, g2, g3):
    row = row_ids()
    return jnp.where(
        row < 4,
        jnp.where(row < 2, g0, pltpu.roll(g1, 2, 0)),
        jnp.where(row < 6, pltpu.roll(g2, 4, 0), pltpu.roll(g3, 6, 0)),
    )


def gather_tile(load, index, tiles, found):
    lane = jnp.broadcast_to(index & 127, (8, LANES))
    tile = jnp.broadcast_to(index >> 7, (8, LANES))
    for k, name in enumerate(tiles):
        here = tile == name
        for g in range(3):
            found[g] = jnp.where(here, jnp.take_along_axis(load(k, g), lane, axis=1), found[g])
    return found


def expand(tiles, indices, highs):
    tops = []
    rests = []
    for tile, index in zip(tiles, indices):
        top = tile.astype(jnp.bfloat16).astype(jnp.float32)
        rest = tile - top
        high = jnp.broadcast_to(index >> 8, tile.shape)
        column = [[], []]
        for k in highs:
            here = high == k
            column[0].append(jnp.where(here, top, 0.0))
            column[1].append(jnp.where(here, rest, 0.0))
        tops.append(jnp.concatenate(column[0], 0).astype(jnp.bfloat16))
        rests.append(jnp.concatenate(column[1], 0).astype(jnp.bfloat16))
    return jnp.concatenate(tops + rests, 1)


def hot_tile(index):
    low = jnp.broadcast_to(index & (LOW - 1), (LOW, LANES))
    hot = lax.broadcasted_iota(jnp.int32, (LOW, LANES), 0) == low
    return hot.astype(jnp.float32).astype(jnp.bfloat16)


def contract(left, hots):
    right = jnp.concatenate(hots + hots, 1)
    return lax.dot_general(
        left, right, (((1,), (1,)), ((), ())), preferred_element_type=jnp.float32
    )


def side_by_side(blocks):
    lane = lane_ids(32)
    out = blocks[0]
    for j in range(1, 4):
        out = jnp.where(lane >= 32 * j, pltpu.roll(blocks[j], 32 * j, 1), out)
    return out


def by_step(source_ref, lines_ref, square_ref):
    for m in range(16):
        lines_ref[2 * m : 2 * m + 2, :] = source_ref[:, m * LANES : (m + 1) * LANES]
    square_ref[:, 0:32] = jnp.transpose(lines_ref[...], (1, 0))
    mixed = side_by_side([square_ref[32 * q : 32 * q + 32, :] for q in range(4)])
    lane = lane_ids(8)
    take = (lane & 3) * 32 + ((lane >> 2) & 15) * 2 + (lane >> 6)
    return jnp.concatenate(
        [jnp.take_along_axis(mixed[8 * j : 8 * j + 8], take, axis=1) for j in range(4)], 0
    )


GROUPS = ((2, 0, 4), (2, 4, 8), (1, 0, 8), (3, 0, 8), (0, 0, 8))
ORDER = (2, 1, 3, 0)
SPLITS = ((2,), (1,), (3, 0))


def kernel(
    cell_hbm,
    pore_hbm,
    request_hbm,
    slot_hbm,
    length_hbm,
    courant_hbm,
    weight_hbm,
    inflow_hbm,
    inter_hbm,
    out_ref,
    cell_ref,
    pore_ref,
    request_in,
    slot_in,
    length_in,
    courant_in,
    weight_in,
    inflow_in,
    inter_in,
    square_i,
    square_f,
    lines_i,
    lines_f,
    request_ref,
    slot_ref,
    weight_ref,
    scale_ref,
    decay_ref,
    span_ref,
    hot_slot,
    hot_request,
    send1,
    recv1,
    send_a,
    recv_a,
    send_b,
    recv_b,
    table,
    state,
    rows,
    acc,
    acc_a,
    acc_b,
    part,
    part_flux,
    got,
    got_flux,
    in_sem,
    own_sem,
    send1_sem,
    recv1_sem,
    send_a_sem,
    recv_a_sem,
    send_b_sem,
    recv_b_sem,
    send3_sem,
    recv3_sem,
    send4_sem,
    recv4_sem,
    send5_sem,
    recv5_sem,
    send6_sem,
    recv6_sem,
    send7_sem,
    recv7_sem,
):
    me = lax.axis_index("grid")
    mine = lax.axis_index("bundle")
    my_y = lax.div(me, 32)
    my_pair = lax.rem(lax.div(me, 4), 8)
    my_seat = lax.rem(me, 4)

    loads = [
        pltpu.make_async_copy(source, target, in_sem.at[j])
        for j, (source, target) in enumerate(
            (
                (request_hbm.at[mine], request_in),
                (cell_hbm, cell_ref),
                (slot_hbm, slot_in),
                (courant_hbm, courant_in),
                (weight_hbm, weight_in),
                (length_hbm, length_in),
                (inflow_hbm, inflow_in),
                (inter_hbm, inter_in),
                (pore_hbm, pore_ref),
            )
        )
    ]
    for load in loads:
        load.start()

    barrier = pltpu.get_barrier_semaphore()

    def greet(k, _):
        pl.semaphore_signal(
            barrier, inc=1, device_id=(lax.rem(me + k, GRID), mine), device_id_type=MESH
        )
        return 0

    lax.fori_loop(1, GRID, greet, 0)
    for k in range(1, BUNDLES):
        pl.semaphore_signal(
            barrier, inc=1, device_id=(me, lax.rem(mine + k, BUNDLES)), device_id_type=MESH
        )

    loads[0].wait()
    square_i[:, 0:32] = jnp.transpose(request_in[...], (1, 0))
    request_ref[...] = side_by_side([square_i[pl.ds(d, 32, stride=4), :] for d in range(4)])
    loads[1].wait()

    def pick(t, _):
        found = gather_tile(
            lambda k, g: cell_ref[8 * g : 8 * g + 8, k * LANES : (k + 1) * LANES],
            request_ref[pl.ds(t, 1), :],
            range(TILES),
            [jnp.zeros((8, LANES), jnp.float32)] * 3,
        )
        blocks = swap_blocks(to_groups(*found))
        for d in range(4):
            send1[t * 4 + d] = blocks[d][:6]
        return 0

    def post_one(source, target, send_sem, recv_sem, peer):
        pltpu.make_async_remote_copy(
            src_ref=source.at[peer],
            dst_ref=target.at[me],
            send_sem=send_sem,
            recv_sem=recv_sem,
            device_id=(peer, mine),
            device_id_type=MESH,
        ).start()

    def hop(j):
        return 4 + lax.div(j + 1, 2) * (1 - 2 * lax.rem(j, 2))

    def tile_to(r, j):
        return lax.rem(my_y + r, 4) * 8 + lax.rem(my_pair + hop(j), 8)

    def post(source, target, send_sem, recv_sems, group):
        r, low, high = GROUPS[group]
        here = r == 0 and high == 8

        def ring(j, _):
            for seat in range(4):
                post_one(source, target, send_sem, recv_sems.at[group], tile_to(r, j) * 4 + seat)
            return 0

        lax.fori_loop(low, high - here, ring, 0)
        if here:
            for seat in range(1, 4):
                peer = tile_to(0, 7) * 4 + lax.rem(my_seat + seat, 4)
                post_one(source, target, send_sem, recv_sems.at[group], peer)
            own = pltpu.make_async_copy(source.at[me], target.at[me], own_sem)
            own.start()
            own.wait()

    def arrived(target, recv_sems, r):
        for group, (offset, low, high) in enumerate(GROUPS):
            if offset == r:
                blocks = pl.ds(0, 4 * (high - low) - (r == 0))
                pltpu.make_async_copy(
                    target.at[blocks], target.at[blocks], recv_sems.at[group]
                ).wait()
        return lax.rem(my_y + 4 - r, 4)

    def sent(source, send_sem):
        blocks = pl.ds(0, GRID - 1)
        pltpu.make_async_copy(source.at[blocks], source.at[blocks], send_sem).wait()

    for group in range(len(GROUPS)):
        r, low, high = GROUPS[group]
        lax.fori_loop(low, high, lambda j, c, r=r: pick(tile_to(r, j), c), 0, unroll=2)
        if group == 0:
            pl.semaphore_wait(barrier, GRID - 1 + BUNDLES - 1)
        post(send1, recv1, send1_sem, recv1_sem, group)

    for load in loads[2:]:
        load.wait()
    slot_ref[...] = by_step(slot_in, lines_i, square_i)
    courant = by_step(courant_in, lines_f, square_f)
    scale = 1.0 / (1.0 + courant)
    scale_ref[...] = scale
    decay_ref[...] = courant * scale
    span_ref[0:1, :] = decay_ref[0:1, :]
    for i in range(1, STEPS):
        span_ref[i : i + 1, :] = span_ref[i - 1 : i, :] * decay_ref[i : i + 1, :]
    flux = by_step(weight_in, lines_f, square_f)
    lane = lane_ids(32)
    node = (lane & (CHUNKS - 1)) * STEPS + row_ids(32)
    first_line = jnp.broadcast_to(length_in[:, 0:1], (32, LANES))
    second_line = jnp.broadcast_to(length_in[:, 1:2], (32, LANES))
    weight_ref[...] = jnp.where(node < jnp.where(lane < CHUNKS, first_line, second_line), flux, 0.0)

    def heat(t, _):
        hot_slot[t] = hot_tile(slot_ref[pl.ds(t, 1), :])
        hot_request[t] = hot_tile(request_ref[pl.ds(t, 1), :])
        return 0

    lax.fori_loop(0, TILES, heat, 0)
    square = lax.broadcasted_iota(jnp.int32, (SPECIES, SPECIES), 0) == lax.broadcasted_iota(
        jnp.int32, (SPECIES, SPECIES), 1
    )
    entry = jnp.sum(
        jnp.where(square, jnp.broadcast_to(inflow_in[...], (SPECIES, SPECIES)), 0.0),
        axis=1,
        keepdims=True,
    )
    entry = jnp.broadcast_to(entry, (SPECIES, LANES))
    square_f[0:SPECIES, :] = jnp.zeros((SPECIES, LANES), jnp.float32)
    square_f[0:SPECIES, 0:SPECIES] = inter_in[...]
    inter = square_f[0:SPECIES, :]
    inter_top = inter.astype(jnp.bfloat16).astype(jnp.float32)
    inter_rest = inter - inter_top
    inter = inter_top + pltpu.roll(inter_top, 32, 1) + pltpu.roll(inter_rest, 64, 1)
    inter = inter.astype(jnp.bfloat16)
    chunk = lane_ids(SPECIES) & (CHUNKS - 1)
    levels = []
    level = jnp.broadcast_to(span_ref[STEPS - 1 : STEPS, :], (SPECIES, LANES))
    span_all = level
    for bit in range(6):
        levels.append(level)
        behind = pltpu.roll(level, 1 << bit, 1)
        level = jnp.where(chunk >= (1 << bit), level * behind, level)

    for step, r in enumerate(ORDER):
        base = arrived(recv1, recv1_sem, r) * 8
        pad = jnp.zeros((2, LANES), jnp.float32)
        for u in range(8):
            parts = [
                jnp.concatenate([recv1[base * 4 + u * 4 + d], pad], 0) for d in range(4)
            ]
            for g, value in enumerate(from_groups(*swap_blocks(parts))):
                table[u, 8 * g : 8 * g + 8, :] = value

        def fetch(t, _, base=base, step=step):
            if step == 0:
                found = [jnp.zeros((8, LANES), jnp.float32)] * 3
            else:
                found = [state[t, 8 * g : 8 * g + 8, :] for g in range(3)]
            found = gather_tile(
                lambda k, g: table[k, 8 * g : 8 * g + 8, :],
                slot_ref[pl.ds(t, 1), :] - base * LANES,
                range(8),
                found,
            )
            for g in range(3):
                state[t, 8 * g : 8 * g + 8, :] = found[g]
            return 0

        lax.fori_loop(0, TILES, fetch, 0, unroll=4)

    def row(ref, i):
        return jnp.broadcast_to(ref[i : i + 1, :], (SPECIES, LANES))

    before = None
    for substep in range(SUB):
        value = jnp.zeros((SPECIES, LANES), jnp.float32)
        for i in range(STEPS):
            held = state[i]
            if substep > 0:
                held = held + row(span_ref, i) * before
            value = row(decay_ref, i) * value + row(scale_ref, i) * held
            state[i] = value
        ends = jnp.where(chunk == 0, value + span_all * entry, value)
        for bit in range(6):
            behind = pltpu.roll(ends, 1 << bit, 1)
            ends = jnp.where(chunk >= (1 << bit), ends + levels[bit] * behind, ends)
        before = jnp.where(chunk == 0, entry, pltpu.roll(ends, 1, 1))
    for i in range(STEPS):
        state[i] = state[i] + row(span_ref, i) * before

    def react(j, _):
        base = jnp.concatenate([state[j * 4 + q] for q in range(4)], 1)
        gap = jnp.zeros((8, 4 * LANES), jnp.float32)
        iterate = base
        for _step in range(NEWTON):
            active = jnp.concatenate([jnp.tanh(iterate), gap], 0)
            top = active.astype(jnp.bfloat16)
            rest = (active - top.astype(jnp.float32)).astype(jnp.bfloat16)
            stack = jnp.concatenate([top, rest, top, jnp.zeros_like(top)], 0)
            iterate = base - jnp.dot(inter, stack, preferred_element_type=jnp.float32)
        for q in range(4):
            weight = jnp.broadcast_to(weight_ref[pl.ds(j * 4 + q, 1), :], (8, LANES))
            result = iterate[:, q * LANES : (q + 1) * LANES]
            for g in range(3):
                rows[j * 4 + q, 8 * g : 8 * g + 8, :] = result[8 * g : 8 * g + 8] * weight
            rows[j * 4 + q, 24:32, :] = jnp.where(row_ids() == 0, weight, 0.0)
        return 0

    lax.fori_loop(0, TILES // 4, react, 0, unroll=4)

    sent(send1, send1_sem)
    for split in SPLITS:
        ys = [lax.rem(my_y + r, 4) for r in split]
        height = 128 * len(split)
        highs = [y * 4 + sub for y in ys for sub in range(4)]
        for j in range(TILES // 4):
            span = range(4 * j, 4 * j + 4)
            left = expand([rows[t] for t in span], [slot_ref[t : t + 1, :] for t in span], highs)
            more = contract(left, [hot_slot[t] for t in span])
            if j == 0:
                acc[0:height, :] = more
            else:
                acc[0:height, :] += more
        for k in range(len(highs)):
            for side in range(2):
                lanes = slice(side * LANES, (side + 1) * LANES)
                blocks = swap_blocks(
                    to_blocks(*[acc[k * 32 + 8 * g : k * 32 + 8 * g + 8, lanes] for g in range(4)])
                )
                for d in range(4):
                    send_a[highs[k] * 8 + side * 4 + d] = blocks[d][:5]
                    send_b[highs[k] * 8 + side * 4 + d] = blocks[d][5:7]
        for group in range(len(GROUPS)):
            if GROUPS[group][0] in split:
                post(send_a, recv_a, send_a_sem, recv_a_sem, group)
    for group in range(len(GROUPS)):
        post(send_b, recv_b, send_b_sem, recv_b_sem, group)

    def collect(target, recv_sems, step, pad_rows, combine, total):
        base = arrived(target, recv_sems, ORDER[step]) * 8
        pad = jnp.zeros((pad_rows, LANES), jnp.float32)
        indices = request_ref[pl.ds(pl.multiple_of(base, 8), 8), :]
        for j in range(2):
            span = range(4 * j, 4 * j + 4)
            tiles = []
            for u in span:
                parts = [
                    jnp.concatenate([target[base * 4 + u * 4 + d], pad], 0) for d in range(4)
                ]
                tiles.append(combine(*swap_blocks(parts)))
            left = expand(tiles, [indices[u : u + 1] for u in span], range(HIGH))
            more = contract(left, [hot_request[base + u] for u in span])
            if step == 0 and j == 0:
                total[...] = more
            else:
                total[...] += more

    def over_bundles(pairs):
        copies = []
        for k in (2, 1, 3):
            peer = lax.rem(mine + k, BUNDLES)
            cells = pl.ds(pl.multiple_of(peer * QUARTER, QUARTER), QUARTER)
            for source, target, sends, recvs in pairs:
                copy = pltpu.make_async_remote_copy(
                    src_ref=source(cells),
                    dst_ref=target(k - 1),
                    send_sem=sends.at[k - 1],
                    recv_sem=recvs.at[k - 1],
                    device_id=(me, peer),
                    device_id_type=MESH,
                )
                copy.start()
                copies.append(copy)
        return copies

    ours = pl.ds(pl.multiple_of(mine * QUARTER, QUARTER), QUARTER)

    def finish(species, sends, recvs):
        total = part[species, ours] + got[0, species] + got[1, species] + got[2, species]
        flux = part_flux[:, ours] + got_flux[0] + got_flux[1] + got_flux[2]
        pore = pore_ref[:, ours]
        out_ref[species, ours] = (pore * cell_ref[species, ours] + total) / (pore + flux)
        return over_bundles(
            [
                (
                    lambda cells: out_ref.at[species, ours],
                    lambda k: out_ref.at[species, ours],
                    sends,
                    recvs,
                )
            ]
        )

    first = slice(0, 16)
    second = slice(16, 24)
    for step in range(4):
        collect(
            recv_a, recv_a_sem, step, 3, lambda *g: jnp.concatenate(from_first(*g), 0), acc_a
        )
    for h in range(HIGH):
        for side in range(2):
            lanes = slice(side * LANES, (side + 1) * LANES)
            cells = slice((h * 2 + side) * LANES, (h * 2 + side + 1) * LANES)
            part[0:16, cells] = acc_a[h * 24 : h * 24 + 16, lanes]
            part_flux[:, cells] = acc_a[h * 24 + 16 : h * 24 + 17, lanes]
    sums_first = over_bundles(
        [
            (lambda cells: part.at[first, cells], lambda k: got.at[k, first], send3_sem, recv3_sem),
            (lambda cells: part_flux.at[:, cells], lambda k: got_flux.at[k], send4_sem, recv4_sem),
        ]
    )

    for step in range(4):
        collect(recv_b, recv_b_sem, step, 6, from_second, acc_b)
    for h in range(HIGH):
        for side in range(2):
            cells = slice((h * 2 + side) * LANES, (h * 2 + side + 1) * LANES)
            part[second, cells] = acc_b[h * 8 : h * 8 + 8, side * LANES : (side + 1) * LANES]
    sums_second = over_bundles(
        [(lambda cells: part.at[second, cells], lambda k: got.at[k, second], send6_sem, recv6_sem)]
    )

    for copy in sums_first:
        copy.wait()
    done = finish(first, send5_sem, recv5_sem)
    for copy in sums_second:
        copy.wait()
    done = done + finish(second, send7_sem, recv7_sem)
    sent(send_a, send_a_sem)
    sent(send_b, send_b_sem)
    for copy in done:
        copy.wait()


def shards(
    cell_state,
    pore_volume,
    request_cell,
    node_slot,
    line_length,
    courant,
    flux_weight,
    inflow,
    interaction,
):
    f32 = jnp.float32
    i32 = jnp.int32
    vmem = pltpu.VMEM
    dma = pltpu.SemaphoreType.DMA
    return pl.pallas_call(
        kernel,
        out_shape=jax.ShapeDtypeStruct((SPECIES, CELLS), f32),
        in_specs=[pl.BlockSpec(memory_space=pltpu.HBM)] * 9,
        out_specs=pl.BlockSpec(memory_space=pltpu.VMEM),
        scratch_shapes=[
            vmem((SPECIES, CELLS), f32),
            vmem((1, CELLS), f32),
            vmem((CAP, GRID), i32),
            vmem((LINES, NODES), i32),
            vmem((1, LINES), i32),
            vmem((LINES, NODES), f32),
            vmem((LINES, NODES), f32),
            vmem((1, SPECIES), f32),
            vmem((SPECIES, SPECIES), f32),
            vmem((LANES, LANES), i32),
            vmem((LANES, LANES), f32),
            vmem((32, LANES), i32),
            vmem((32, LANES), f32),
            vmem((32, LANES), i32),
            vmem((32, LANES), i32),
            vmem((32, LANES), f32),
            vmem((32, LANES), f32),
            vmem((32, LANES), f32),
            vmem((32, LANES), f32),
            vmem((TILES, LOW, LANES), jnp.bfloat16),
            vmem((TILES, LOW, LANES), jnp.bfloat16),
            vmem((GRID, 6, LANES), f32),
            vmem((GRID, 6, LANES), f32),
            vmem((GRID, 5, LANES), f32),
            vmem((GRID, 5, LANES), f32),
            vmem((GRID, 2, LANES), f32),
            vmem((GRID, 2, LANES), f32),
            vmem((8, SPECIES, LANES), f32),
            vmem((TILES, SPECIES, LANES), f32),
            vmem((TILES, 32, LANES), f32),
            vmem((LOW, LOW), f32),
            vmem((HIGH * 24, LOW), f32),
            vmem((HIGH * 8, LOW), f32),
            vmem((SPECIES, CELLS), f32),
            vmem((1, CELLS), f32),
            vmem((BUNDLES - 1, SPECIES, QUARTER), f32),
            vmem((BUNDLES - 1, 1, QUARTER), f32),
            dma((9,)),
            dma,
            dma,
            dma((len(GROUPS),)),
            dma,
            dma((len(GROUPS),)),
            dma,
            dma((len(GROUPS),)),
            dma((3,)),
            dma((3,)),
            dma((3,)),
            dma((3,)),
            dma((3,)),
            dma((3,)),
            dma((3,)),
            dma((3,)),
            dma((3,)),
            dma((3,)),
        ],
        compiler_params=pltpu.CompilerParams(
            collective_id=0, has_side_effects=True, vmem_limit_bytes=20 << 20
        ),
        name="streamlines",
    )(
        *[
            pltpu.with_memory_space_constraint(x, pltpu.HBM)
            for x in (
                cell_state,
                pore_volume.reshape(1, CELLS),
                jnp.transpose(request_cell[:, 0], (0, 2, 1)),
                node_slot[0],
                line_length,
                courant[0],
                flux_weight[0],
                inflow,
                interaction,
            )
        ]
    )


def solution(mesh):
    placed = (
        P(None, "grid"),
        P("grid"),
        P(None, "grid", None, None),
        P("bundle", "grid", None),
        P("bundle", "grid"),
        P("bundle", "grid", None),
        P("bundle", "grid", None),
        P("bundle", None),
        P(),
    )
    return jax.shard_map(
        shards, mesh=mesh, in_specs=placed, out_specs=P(None, "grid"), check_vma=False
    )
```

```python
import jax
import jax.numpy as jnp
from jax import lax
from jax.experimental import pallas as pl
from jax.experimental.pallas import tpu as pltpu
from jax.sharding import PartitionSpec as P

SUB = 2
NEWTON = 3
SPECIES = 24
CELLS = 4096
SLOTS = 4096
NODES = 2048
LINES = 2
GRID = 128
BUNDLES = 4
CAP = 32
CHUNKS = 64
STEPS = NODES // CHUNKS
TILES = 32
LANES = 128
LOW = 256
HIGH = 16
QUARTER = CELLS // BUNDLES
MESH = pl.DeviceIdType.MESH


def lane_ids(rows):
    return lax.broadcasted_iota(jnp.int32, (rows, LANES), 1)


def row_ids(rows=8):
    return lax.broadcasted_iota(jnp.int32, (rows, LANES), 0)


def swap_blocks(parts):
    lane = lane_ids(parts[0].shape[0])
    far = lane < 64
    near = (lane & 32) == 0
    a, b, c, d = parts
    a, c = jnp.where(far, a, pltpu.roll(c, 64, 1)), jnp.where(far, pltpu.roll(a, 64, 1), c)
    b, d = jnp.where(far, b, pltpu.roll(d, 64, 1)), jnp.where(far, pltpu.roll(b, 64, 1), d)
    a, b = jnp.where(near, a, pltpu.roll(b, 32, 1)), jnp.where(near, pltpu.roll(a, 96, 1), b)
    c, d = jnp.where(near, c, pltpu.roll(d, 32, 1)), jnp.where(near, pltpu.roll(c, 96, 1), d)
    return a, b, c, d


def to_groups(v0, v1, v2):
    row = row_ids()
    last = jnp.where(
        row < 2,
        pltpu.roll(v0, 2, 0),
        jnp.where(row < 4, pltpu.roll(v1, 4, 0), pltpu.roll(v2, 6, 0)),
    )
    return v0, v1, v2, last


def from_groups(g0, g1, g2, g3):
    row = row_ids()
    low = row < 6
    return (
        jnp.where(low, g0, pltpu.roll(g3, 6, 0)),
        jnp.where(low, g1, pltpu.roll(g3, 4, 0)),
        jnp.where(low, g2, pltpu.roll(g3, 2, 0)),
    )


def to_blocks(v0, v1, v2, flux):
    row = row_ids()
    head = row < 5
    return (
        jnp.where(head, v0, pltpu.roll(v2, 5, 0)),
        jnp.where(head, v1, pltpu.roll(v2, 3, 0)),
        jnp.where(
            row < 3,
            pltpu.roll(v0, 3, 0),
            jnp.where(head, pltpu.roll(v1, 6, 0), pltpu.roll(v2, 1, 0)),
        ),
        jnp.where(
            row < 1,
            pltpu.roll(v1, 1, 0),
            jnp.where(head, pltpu.roll(flux, 1, 0), pltpu.roll(v2, 7, 0)),
        ),
    )


def from_first(g0, g1, g2, g3):
    row = row_ids()
    head = row < 5
    return (
        jnp.where(head, g0, pltpu.roll(g2, 5, 0)),
        jnp.where(head, g1, jnp.where(row < 7, pltpu.roll(g2, 2, 0), pltpu.roll(g3, 7, 0))),
        jnp.where(row < 1, pltpu.roll(g3, 7, 0), 0.0),
    )


def from_second(g0, g1, g2, g3):
    row = row_ids()
    return jnp.where(
        row < 4,
        jnp.where(row < 2, g0, pltpu.roll(g1, 2, 0)),
        jnp.where(row < 6, pltpu.roll(g2, 4, 0), pltpu.roll(g3, 6, 0)),
    )


def gather_tile(load, index, tiles, found):
    lane = jnp.broadcast_to(index & 127, (8, LANES))
    tile = jnp.broadcast_to(index >> 7, (8, LANES))
    for k, name in enumerate(tiles):
        here = tile == name
        for g in range(3):
            found[g] = jnp.where(here, jnp.take_along_axis(load(k, g), lane, axis=1), found[g])
    return found


def expand(tiles, indices, highs):
    tops = []
    rests = []
    for tile, index in zip(tiles, indices):
        top = tile.astype(jnp.bfloat16).astype(jnp.float32)
        rest = tile - top
        high = jnp.broadcast_to(index >> 8, tile.shape)
        column = [[], []]
        for k in highs:
            here = high == k
            column[0].append(jnp.where(here, top, 0.0))
            column[1].append(jnp.where(here, rest, 0.0))
        tops.append(jnp.concatenate(column[0], 0).astype(jnp.bfloat16))
        rests.append(jnp.concatenate(column[1], 0).astype(jnp.bfloat16))
    return jnp.concatenate(tops + rests, 1)


def hot_tile(index):
    low = jnp.broadcast_to(index & (LOW - 1), (LOW, LANES))
    hot = lax.broadcasted_iota(jnp.int32, (LOW, LANES), 0) == low
    return hot.astype(jnp.float32).astype(jnp.bfloat16)


def contract(left, hots):
    right = jnp.concatenate(hots + hots, 1)
    return lax.dot_general(
        left, right, (((1,), (1,)), ((), ())), preferred_element_type=jnp.float32
    )


def side_by_side(blocks):
    lane = lane_ids(32)
    out = blocks[0]
    for j in range(1, 4):
        out = jnp.where(lane >= 32 * j, pltpu.roll(blocks[j], 32 * j, 1), out)
    return out


def by_step(source_ref, lines_ref, square_ref):
    for m in range(16):
        lines_ref[2 * m : 2 * m + 2, :] = source_ref[:, m * LANES : (m + 1) * LANES]
    square_ref[:, 0:32] = jnp.transpose(lines_ref[...], (1, 0))
    mixed = side_by_side([square_ref[32 * q : 32 * q + 32, :] for q in range(4)])
    lane = lane_ids(8)
    take = (lane & 3) * 32 + ((lane >> 2) & 15) * 2 + (lane >> 6)
    return jnp.concatenate(
        [jnp.take_along_axis(mixed[8 * j : 8 * j + 8], take, axis=1) for j in range(4)], 0
    )


GROUPS = ((2, 0, 4), (2, 4, 8), (1, 0, 8), (3, 0, 8), (0, 0, 8))
ORDER = (2, 1, 3, 0)
SPLITS = ((2,), (1,), (3, 0))


def kernel(
    cell_hbm,
    pore_hbm,
    request_hbm,
    slot_hbm,
    length_hbm,
    courant_hbm,
    weight_hbm,
    inflow_hbm,
    inter_hbm,
    out_ref,
    cell_ref,
    pore_ref,
    request_in,
    slot_in,
    length_in,
    courant_in,
    weight_in,
    inflow_in,
    inter_in,
    square_i,
    square_f,
    lines_i,
    lines_f,
    request_ref,
    slot_ref,
    weight_ref,
    scale_ref,
    decay_ref,
    span_ref,
    hot_slot,
    hot_request,
    send1,
    recv1,
    send_a,
    recv_a,
    send_b,
    recv_b,
    table,
    state,
    rows,
    acc,
    acc_a,
    acc_b,
    part,
    part_flux,
    got,
    got_flux,
    in_sem,
    own_sem,
    send1_sem,
    recv1_sem,
    send_a_sem,
    recv_a_sem,
    send_b_sem,
    recv_b_sem,
    send3_sem,
    recv3_sem,
    send4_sem,
    recv4_sem,
    send5_sem,
    recv5_sem,
    send6_sem,
    recv6_sem,
    send7_sem,
    recv7_sem,
):
    me = lax.axis_index("grid")
    mine = lax.axis_index("bundle")
    my_y = lax.div(me, 32)
    my_pair = lax.rem(lax.div(me, 4), 8)
    my_seat = lax.rem(me, 4)

    loads = [
        pltpu.make_async_copy(source, target, in_sem.at[j])
        for j, (source, target) in enumerate(
            (
                (request_hbm.at[mine], request_in),
                (cell_hbm, cell_ref),
                (slot_hbm, slot_in),
                (courant_hbm, courant_in),
                (weight_hbm, weight_in),
                (length_hbm, length_in),
                (inflow_hbm, inflow_in),
                (inter_hbm, inter_in),
                (pore_hbm, pore_ref),
            )
        )
    ]
    for load in loads[:2]:
        load.start()

    barrier = pltpu.get_barrier_semaphore()

    def hop(j):
        return 4 + lax.div(j + 1, 2) * (1 - 2 * lax.rem(j, 2))

    def tile_to(r, j):
        return lax.rem(my_y + r, 4) * 8 + lax.rem(my_pair + hop(j), 8)

    def signal(peer):
        pl.semaphore_signal(barrier, inc=1, device_id=(peer, mine), device_id_type=MESH)

    for r in ORDER:

        def greet(j, _, r=r):
            for seat in range(4):
                signal(tile_to(r, j) * 4 + seat)
            return 0

        lax.fori_loop(0, 8 if r else 7, greet, 0)
    for seat in range(1, 4):
        signal(tile_to(0, 7) * 4 + lax.rem(my_seat + seat, 4))
    for k in range(1, BUNDLES):
        pl.semaphore_signal(
            barrier, inc=1, device_id=(me, lax.rem(mine + k, BUNDLES)), device_id_type=MESH
        )

    for load in loads[2:]:
        load.start()

    loads[0].wait()
    square_i[:, 0:32] = jnp.transpose(request_in[...], (1, 0))
    request_ref[...] = side_by_side([square_i[pl.ds(d, 32, stride=4), :] for d in range(4)])
    loads[1].wait()

    def pick(t, _):
        found = gather_tile(
            lambda k, g: cell_ref[8 * g : 8 * g + 8, k * LANES : (k + 1) * LANES],
            request_ref[pl.ds(t, 1), :],
            range(TILES),
            [jnp.zeros((8, LANES), jnp.float32)] * 3,
        )
        blocks = swap_blocks(to_groups(*found))
        for d in range(4):
            send1[t * 4 + d] = blocks[d][:6]
        return 0

    def post_one(source, target, send_sem, recv_sem, peer):
        pltpu.make_async_remote_copy(
            src_ref=source.at[peer],
            dst_ref=target.at[me],
            send_sem=send_sem,
            recv_sem=recv_sem,
            device_id=(peer, mine),
            device_id_type=MESH,
        ).start()

    def post(source, target, send_sem, recv_sems, group):
        r, low, high = GROUPS[group]
        here = r == 0 and high == 8

        def ring(j, _):
            for seat in range(4):
                post_one(source, target, send_sem, recv_sems.at[group], tile_to(r, j) * 4 + seat)
            return 0

        lax.fori_loop(low, high - here, ring, 0)
        if here:
            for seat in range(1, 4):
                peer = tile_to(0, 7) * 4 + lax.rem(my_seat + seat, 4)
                post_one(source, target, send_sem, recv_sems.at[group], peer)
            own = pltpu.make_async_copy(source.at[me], target.at[me], own_sem)
            own.start()
            own.wait()

    def arrived(target, recv_sems, r):
        for group, (offset, low, high) in enumerate(GROUPS):
            if offset == r:
                blocks = pl.ds(0, 4 * (high - low) - (r == 0))
                pltpu.make_async_copy(
                    target.at[blocks], target.at[blocks], recv_sems.at[group]
                ).wait()
        return lax.rem(my_y + 4 - r, 4)

    def sent(source, send_sem):
        blocks = pl.ds(0, GRID - 1)
        pltpu.make_async_copy(source.at[blocks], source.at[blocks], send_sem).wait()

    for group in range(len(GROUPS)):
        r, low, high = GROUPS[group]
        lax.fori_loop(low, high, lambda j, c, r=r: pick(tile_to(r, j), c), 0, unroll=2)
        if group == 0:
            pl.semaphore_wait(barrier, GRID - 1 + BUNDLES - 1)
        post(send1, recv1, send1_sem, recv1_sem, group)

    for load in loads[2:]:
        load.wait()
    slot_ref[...] = by_step(slot_in, lines_i, square_i)
    courant = by_step(courant_in, lines_f, square_f)
    scale = 1.0 / (1.0 + courant)
    scale_ref[...] = scale
    decay_ref[...] = courant * scale
    span_ref[0:1, :] = decay_ref[0:1, :]
    for i in range(1, STEPS):
        span_ref[i : i + 1, :] = span_ref[i - 1 : i, :] * decay_ref[i : i + 1, :]
    flux = by_step(weight_in, lines_f, square_f)
    lane = lane_ids(32)
    node = (lane & (CHUNKS - 1)) * STEPS + row_ids(32)
    first_line = jnp.broadcast_to(length_in[:, 0:1], (32, LANES))
    second_line = jnp.broadcast_to(length_in[:, 1:2], (32, LANES))
    weight_ref[...] = jnp.where(node < jnp.where(lane < CHUNKS, first_line, second_line), flux, 0.0)

    def heat(t, _):
        hot_slot[t] = hot_tile(slot_ref[pl.ds(t, 1), :])
        hot_request[t] = hot_tile(request_ref[pl.ds(t, 1), :])
        return 0

    lax.fori_loop(0, TILES, heat, 0)
    square = lax.broadcasted_iota(jnp.int32, (SPECIES, SPECIES), 0) == lax.broadcasted_iota(
        jnp.int32, (SPECIES, SPECIES), 1
    )
    entry = jnp.sum(
        jnp.where(square, jnp.broadcast_to(inflow_in[...], (SPECIES, SPECIES)), 0.0),
        axis=1,
        keepdims=True,
    )
    entry = jnp.broadcast_to(entry, (SPECIES, LANES))
    square_f[0:SPECIES, :] = jnp.zeros((SPECIES, LANES), jnp.float32)
    square_f[0:SPECIES, 0:SPECIES] = inter_in[...]
    inter = square_f[0:SPECIES, :]
    inter_top = inter.astype(jnp.bfloat16).astype(jnp.float32)
    inter_rest = inter - inter_top
    inter = inter_top + pltpu.roll(inter_top, 32, 1) + pltpu.roll(inter_rest, 64, 1)
    inter = inter.astype(jnp.bfloat16)
    chunk = lane_ids(SPECIES) & (CHUNKS - 1)
    levels = []
    level = jnp.broadcast_to(span_ref[STEPS - 1 : STEPS, :], (SPECIES, LANES))
    span_all = level
    for bit in range(6):
        levels.append(level)
        behind = pltpu.roll(level, 1 << bit, 1)
        level = jnp.where(chunk >= (1 << bit), level * behind, level)

    for step, r in enumerate(ORDER):
        base = arrived(recv1, recv1_sem, r) * 8
        pad = jnp.zeros((2, LANES), jnp.float32)
        for u in range(8):
            parts = [
                jnp.concatenate([recv1[base * 4 + u * 4 + d], pad], 0) for d in range(4)
            ]
            for g, value in enumerate(from_groups(*swap_blocks(parts))):
                table[u, 8 * g : 8 * g + 8, :] = value

        def fetch(t, _, base=base, step=step):
            if step == 0:
                found = [jnp.zeros((8, LANES), jnp.float32)] * 3
            else:
                found = [state[t, 8 * g : 8 * g + 8, :] for g in range(3)]
            found = gather_tile(
                lambda k, g: table[k, 8 * g : 8 * g + 8, :],
                slot_ref[pl.ds(t, 1), :] - base * LANES,
                range(8),
                found,
            )
            for g in range(3):
                state[t, 8 * g : 8 * g + 8, :] = found[g]
            return 0

        lax.fori_loop(0, TILES, fetch, 0, unroll=4)

    def row(ref, i):
        return jnp.broadcast_to(ref[i : i + 1, :], (SPECIES, LANES))

    before = None
    for substep in range(SUB):
        value = jnp.zeros((SPECIES, LANES), jnp.float32)
        for i in range(STEPS):
            held = state[i]
            if substep > 0:
                held = held + row(span_ref, i) * before
            value = row(decay_ref, i) * value + row(scale_ref, i) * held
            state[i] = value
        ends = jnp.where(chunk == 0, value + span_all * entry, value)
        for bit in range(6):
            behind = pltpu.roll(ends, 1 << bit, 1)
            ends = jnp.where(chunk >= (1 << bit), ends + levels[bit] * behind, ends)
        before = jnp.where(chunk == 0, entry, pltpu.roll(ends, 1, 1))
    for i in range(STEPS):
        state[i] = state[i] + row(span_ref, i) * before

    def react(j, _):
        base = jnp.concatenate([state[j * 4 + q] for q in range(4)], 1)
        gap = jnp.zeros((8, 4 * LANES), jnp.float32)
        iterate = base
        for _step in range(NEWTON):
            active = jnp.concatenate([jnp.tanh(iterate), gap], 0)
            top = active.astype(jnp.bfloat16)
            rest = (active - top.astype(jnp.float32)).astype(jnp.bfloat16)
            stack = jnp.concatenate([top, rest, top, jnp.zeros_like(top)], 0)
            iterate = base - jnp.dot(inter, stack, preferred_element_type=jnp.float32)
        for q in range(4):
            weight = jnp.broadcast_to(weight_ref[pl.ds(j * 4 + q, 1), :], (8, LANES))
            result = iterate[:, q * LANES : (q + 1) * LANES]
            for g in range(3):
                rows[j * 4 + q, 8 * g : 8 * g + 8, :] = result[8 * g : 8 * g + 8] * weight
            rows[j * 4 + q, 24:32, :] = jnp.where(row_ids() == 0, weight, 0.0)
        return 0

    lax.fori_loop(0, TILES // 4, react, 0, unroll=4)

    sent(send1, send1_sem)
    for split in SPLITS:
        ys = [lax.rem(my_y + r, 4) for r in split]
        height = 128 * len(split)
        highs = [y * 4 + sub for y in ys for sub in range(4)]
        for j in range(TILES // 4):
            span = range(4 * j, 4 * j + 4)
            left = expand([rows[t] for t in span], [slot_ref[t : t + 1, :] for t in span], highs)
            more = contract(left, [hot_slot[t] for t in span])
            if j == 0:
                acc[0:height, :] = more
            else:
                acc[0:height, :] += more
        for k in range(len(highs)):
            for side in range(2):
                lanes = slice(side * LANES, (side + 1) * LANES)
                blocks = swap_blocks(
                    to_blocks(*[acc[k * 32 + 8 * g : k * 32 + 8 * g + 8, lanes] for g in range(4)])
                )
                for d in range(4):
                    send_a[highs[k] * 8 + side * 4 + d] = blocks[d][:5]
                    send_b[highs[k] * 8 + side * 4 + d] = blocks[d][5:7]
        for group in range(len(GROUPS)):
            if GROUPS[group][0] in split:
                post(send_a, recv_a, send_a_sem, recv_a_sem, group)
    for group in range(len(GROUPS)):
        post(send_b, recv_b, send_b_sem, recv_b_sem, group)

    def collect(target, recv_sems, step, pad_rows, combine, total):
        base = arrived(target, recv_sems, ORDER[step]) * 8
        pad = jnp.zeros((pad_rows, LANES), jnp.float32)
        indices = request_ref[pl.ds(pl.multiple_of(base, 8), 8), :]
        for j in range(2):
            span = range(4 * j, 4 * j + 4)
            tiles = []
            for u in span:
                parts = [
                    jnp.concatenate([target[base * 4 + u * 4 + d], pad], 0) for d in range(4)
                ]
                tiles.append(combine(*swap_blocks(parts)))
            left = expand(tiles, [indices[u : u + 1] for u in span], range(HIGH))
            more = contract(left, [hot_request[base + u] for u in span])
            if step == 0 and j == 0:
                total[...] = more
            else:
                total[...] += more

    def over_bundles(pairs):
        copies = []
        for k in (2, 1, 3):
            peer = lax.rem(mine + k, BUNDLES)
            cells = pl.ds(pl.multiple_of(peer * QUARTER, QUARTER), QUARTER)
            for source, target, sends, recvs in pairs:
                copy = pltpu.make_async_remote_copy(
                    src_ref=source(cells),
                    dst_ref=target(k - 1),
                    send_sem=sends.at[k - 1],
                    recv_sem=recvs.at[k - 1],
                    device_id=(me, peer),
                    device_id_type=MESH,
                )
                copy.start()
                copies.append(copy)
        return copies

    ours = pl.ds(pl.multiple_of(mine * QUARTER, QUARTER), QUARTER)

    def finish(species, sends, recvs):
        total = part[species, ours] + got[0, species] + got[1, species] + got[2, species]
        flux = part_flux[:, ours] + got_flux[0] + got_flux[1] + got_flux[2]
        pore = pore_ref[:, ours]
        out_ref[species, ours] = (pore * cell_ref[species, ours] + total) / (pore + flux)
        return over_bundles(
            [
                (
                    lambda cells: out_ref.at[species, ours],
                    lambda k: out_ref.at[species, ours],
                    sends,
                    recvs,
                )
            ]
        )

    first = slice(0, 16)
    second = slice(16, 24)
    for step in range(4):
        collect(
            recv_a, recv_a_sem, step, 3, lambda *g: jnp.concatenate(from_first(*g), 0), acc_a
        )
    for h in range(HIGH):
        for side in range(2):
            lanes = slice(side * LANES, (side + 1) * LANES)
            cells = slice((h * 2 + side) * LANES, (h * 2 + side + 1) * LANES)
            part[0:16, cells] = acc_a[h * 24 : h * 24 + 16, lanes]
            part_flux[:, cells] = acc_a[h * 24 + 16 : h * 24 + 17, lanes]
    sums_first = over_bundles(
        [
            (lambda cells: part.at[first, cells], lambda k: got.at[k, first], send3_sem, recv3_sem),
            (lambda cells: part_flux.at[:, cells], lambda k: got_flux.at[k], send4_sem, recv4_sem),
        ]
    )

    for step in range(4):
        collect(recv_b, recv_b_sem, step, 6, from_second, acc_b)
    for h in range(HIGH):
        for side in range(2):
            cells = slice((h * 2 + side) * LANES, (h * 2 + side + 1) * LANES)
            part[second, cells] = acc_b[h * 8 : h * 8 + 8, side * LANES : (side + 1) * LANES]
    sums_second = over_bundles(
        [(lambda cells: part.at[second, cells], lambda k: got.at[k, second], send6_sem, recv6_sem)]
    )

    for copy in sums_first:
        copy.wait()
    done = finish(first, send5_sem, recv5_sem)
    for copy in sums_second:
        copy.wait()
    done = done + finish(second, send7_sem, recv7_sem)
    sent(send_a, send_a_sem)
    sent(send_b, send_b_sem)
    for copy in done:
        copy.wait()


def shards(
    cell_state,
    pore_volume,
    request_cell,
    node_slot,
    line_length,
    courant,
    flux_weight,
    inflow,
    interaction,
):
    f32 = jnp.float32
    i32 = jnp.int32
    vmem = pltpu.VMEM
    dma = pltpu.SemaphoreType.DMA
    return pl.pallas_call(
        kernel,
        out_shape=jax.ShapeDtypeStruct((SPECIES, CELLS), f32),
        in_specs=[pl.BlockSpec(memory_space=pltpu.HBM)] * 9,
        out_specs=pl.BlockSpec(memory_space=pltpu.VMEM),
        scratch_shapes=[
            vmem((SPECIES, CELLS), f32),
            vmem((1, CELLS), f32),
            vmem((CAP, GRID), i32),
            vmem((LINES, NODES), i32),
            vmem((1, LINES), i32),
            vmem((LINES, NODES), f32),
            vmem((LINES, NODES), f32),
            vmem((1, SPECIES), f32),
            vmem((SPECIES, SPECIES), f32),
            vmem((LANES, LANES), i32),
            vmem((LANES, LANES), f32),
            vmem((32, LANES), i32),
            vmem((32, LANES), f32),
            vmem((32, LANES), i32),
            vmem((32, LANES), i32),
            vmem((32, LANES), f32),
            vmem((32, LANES), f32),
            vmem((32, LANES), f32),
            vmem((32, LANES), f32),
            vmem((TILES, LOW, LANES), jnp.bfloat16),
            vmem((TILES, LOW, LANES), jnp.bfloat16),
            vmem((GRID, 6, LANES), f32),
            vmem((GRID, 6, LANES), f32),
            vmem((GRID, 5, LANES), f32),
            vmem((GRID, 5, LANES), f32),
            vmem((GRID, 2, LANES), f32),
            vmem((GRID, 2, LANES), f32),
            vmem((8, SPECIES, LANES), f32),
            vmem((TILES, SPECIES, LANES), f32),
            vmem((TILES, 32, LANES), f32),
            vmem((LOW, LOW), f32),
            vmem((HIGH * 24, LOW), f32),
            vmem((HIGH * 8, LOW), f32),
            vmem((SPECIES, CELLS), f32),
            vmem((1, CELLS), f32),
            vmem((BUNDLES - 1, SPECIES, QUARTER), f32),
            vmem((BUNDLES - 1, 1, QUARTER), f32),
            dma((9,)),
            dma,
            dma,
            dma((len(GROUPS),)),
            dma,
            dma((len(GROUPS),)),
            dma,
            dma((len(GROUPS),)),
            dma((3,)),
            dma((3,)),
            dma((3,)),
            dma((3,)),
            dma((3,)),
            dma((3,)),
            dma((3,)),
            dma((3,)),
            dma((3,)),
            dma((3,)),
        ],
        compiler_params=pltpu.CompilerParams(
            collective_id=0, has_side_effects=True, vmem_limit_bytes=20 << 20
        ),
        name="streamlines",
    )(
        *[
            pltpu.with_memory_space_constraint(x, pltpu.HBM)
            for x in (
                cell_state,
                pore_volume.reshape(1, CELLS),
                jnp.transpose(request_cell[:, 0], (0, 2, 1)),
                node_slot[0],
                line_length,
                courant[0],
                flux_weight[0],
                inflow,
                interaction,
            )
        ]
    )


def solution(mesh):
    placed = (
        P(None, "grid"),
        P("grid"),
        P(None, "grid", None, None),
        P("bundle", "grid", None),
        P("bundle", "grid"),
        P("bundle", "grid", None),
        P("bundle", "grid", None),
        P("bundle", None),
        P(),
    )
    return jax.shard_map(
        shards, mesh=mesh, in_specs=placed, out_specs=P(None, "grid"), check_vma=False
    )
```
